32 devices in a mesh: gx: 4 (over x, core), gy: 8 (over z, y).
Axes of the slice: x: 2, y: 2, z: 4, core: 2. Of those that a mesh axis runs over, the one named last changes fastest.
Arguments:
- right_side: float32 [32, 64, 512], P('gx', 'gy'), may hold values from -18 to 18
- inverse_density: float32 [32, 64, 512], P('gx', 'gy'), may hold values from 0.01 to 10
Outputs:
- correction: float32 [32, 64, 512], P('gx', 'gy')
- residual: float32 [32, 64, 512], P('gx', 'gy')
The draws below stay inside these ranges and needn't reach their ends.
All inputs are finite; a program needn't handle non-finite values.
Results may differ from the reference program's by a relative error of at most 0.00013.
Values sent between devices are 32-bit elements; how exact they have to be, the bound alone decides.
A program may use at most 64 MiB of HBM per device.

```python
import math
import jax
import jax.numpy as jnp
from jax import lax

CZ = 512
SWEEPS = 2
COARSE_SWEEPS = 8
NX = 32
NY = 64


def steps_of(rng, shape, pieces, low, largest):
    loudness = 1.0
    for position, shards_of in pieces:
        draws = jax.random.uniform(jax.random.fold_in(jax.random.fold_in(rng, 6), position), (shards_of,), jnp.float32, low / len(pieces), largest / len(pieces))
        loudness = loudness * jnp.repeat(jnp.exp(draws), shape[position] // shards_of).reshape((-1,) + (1,) * (len(shape) - 1 - position))
    return loudness


def gaussian(rng, extent, width, bound, pieces=(), kind=jnp.bfloat16):
    array = jax.random.normal(rng, extent, jnp.float32) * width
    if len(pieces) > 0:
        array = steps_of(rng, extent, pieces, -0.22, 0.18) * array
    return jnp.clip(array, min=-bound, max=bound).astype(kind)


def setup_inputs(seed: int = 0) -> dict:
    key_list = jax.random.split(jax.random.key(seed), 3)
    right_side = gaussian(key_list[0], (NX, NY, CZ), 3.0, 18.0, ((0, 4), (1, 8)), jnp.float32)
    inverse_density = jnp.clip(jnp.exp(math.log(10.0) - 6.9077553 * jax.random.uniform(key_list[1], (NX, NY, CZ), jnp.float32) ** steps_of(key_list[1], (NX, NY, CZ), ((0, 4), (1, 8)), -0.2, 0.2)), 0.01, 10.0)
    return {"right_side": right_side, "inverse_density": inverse_density}


def shift_down(values):
    return jnp.pad(values, ((0, 0), (0, 0), (1, 0)))[:, :, :-1]


def shift_up(values):
    return jnp.pad(values, ((0, 0), (0, 0), (0, 1)))[:, :, 1:]


def pad_plane(values):
    return jnp.pad(values, ((1, 1), (1, 1), (0, 0)))


def face_coefs(padded, scale):
    centre = padded[1:-1, 1:-1]
    faces = (
        scale * 0.5 * (centre + padded[:-2, 1:-1]),
        scale * 0.5 * (centre + padded[2:, 1:-1]),
        scale * 0.5 * (centre + padded[1:-1, :-2]),
        scale * 0.5 * (centre + padded[1:-1, 2:]),
        scale * 0.5 * (centre + shift_down(centre)),
        scale * 0.5 * (centre + shift_up(centre)),
    )
    diagonal = faces[0] + faces[1] + faces[2] + faces[3] + faces[4] + faces[5]
    return faces, diagonal


def neighbours(padded, faces):
    centre = padded[1:-1, 1:-1]
    total = faces[0] * padded[:-2, 1:-1] + faces[1] * padded[2:, 1:-1]
    total = total + faces[2] * padded[1:-1, :-2] + faces[3] * padded[1:-1, 2:]
    total = total + faces[4] * shift_down(centre) + faces[5] * shift_up(centre)
    return total


def red_cells(shape):
    along_x = lax.broadcasted_iota(jnp.int32, shape, 0)
    along_y = lax.broadcasted_iota(jnp.int32, shape, 1)
    along_z = lax.broadcasted_iota(jnp.int32, shape, 2)
    return (along_x + along_y + along_z) % 2 == 0


def smooth(field, source, faces, diagonal, sweeps):
    red = red_cells(field.shape)
    for sweep in range(sweeps):
        for colour in (red, jnp.logical_not(red)):
            update = (source + neighbours(pad_plane(field), faces)) / diagonal
            field = jnp.where(colour, update, field)
    return field


def apply_residual(field, source, faces, diagonal):
    return source - (diagonal * field - neighbours(pad_plane(field), faces))


def restrict(values):
    size_x, size_y, size_z = values.shape
    blocks = values.reshape(size_x // 2, 2, size_y // 2, 2, size_z // 2, 2)
    return jnp.mean(blocks, axis=(1, 3, 5))


def prolong(values):
    return jnp.repeat(jnp.repeat(jnp.repeat(values, 2, axis=0), 2, axis=1), 2, axis=2)


def reference(right_side, inverse_density):
    level_one = restrict(inverse_density)
    level_two = restrict(level_one)
    faces_zero, diag_zero = face_coefs(pad_plane(inverse_density), 1.0)
    faces_one, diag_one = face_coefs(pad_plane(level_one), 0.25)
    faces_two, diag_two = face_coefs(pad_plane(level_two), 0.0625)
    fine = smooth(jnp.zeros_like(right_side), right_side, faces_zero, diag_zero, SWEEPS)
    source_one = restrict(apply_residual(fine, right_side, faces_zero, diag_zero))
    middle = smooth(jnp.zeros_like(source_one), source_one, faces_one, diag_one, SWEEPS)
    source_two = restrict(apply_residual(middle, source_one, faces_one, diag_one))
    coarse = smooth(jnp.zeros_like(source_two), source_two, faces_two, diag_two, COARSE_SWEEPS)
    middle = smooth(middle + prolong(coarse), source_one, faces_one, diag_one, SWEEPS)
    fine = smooth(fine + prolong(middle), right_side, faces_zero, diag_zero, SWEEPS)
    return fine, apply_residual(fine, right_side, faces_zero, diag_zero)
```

```python
import functools

import jax
import jax.numpy as jnp
from jax import lax
from jax.experimental import pallas as pl
from jax.experimental.pallas import tpu as pltpu
from jax.sharding import PartitionSpec as P

SWEEPS = 2
COARSE_SWEEPS = 8
MESH = pl.DeviceIdType.MESH
LANES = 128
F32 = jnp.float32


def iota(shape, dim):
    return lax.broadcasted_iota(jnp.int32, shape, dim)


def lane_prev(a):
    return jnp.where(iota(a.shape, 2) == 0, 0.0, pltpu.roll(a, 1, 2))


def lane_next(a):
    return jnp.where(iota(a.shape, 2) == LANES - 1, 0.0, pltpu.roll(a, LANES - 1, 2))


def row_prev(a, halo):
    return jnp.where(iota(a.shape, 1) == 0, halo, pltpu.roll(a, 1, 1)) if a.shape[1] % 8 == 0 else jnp.concatenate(
        [halo, a[:, :-1]], axis=1
    )


def row_next(a, halo):
    rows = a.shape[1]
    return jnp.where(iota(a.shape, 1) == rows - 1, halo, pltpu.roll(a, rows - 1, 1)) if rows % 8 == 0 else jnp.concatenate(
        [a[:, 1:], halo], axis=1
    )


def even_cells(shape):
    return (iota(shape, 0) + iota(shape, 1)) % 2 == 0


def z_other(o, colour):
    even = even_cells(o[0].shape)
    low = even if colour == 0 else jnp.logical_not(even)
    last = len(o) - 1
    out = []
    for b in range(last + 1):
        before = o[b - 1] if b > 0 else lane_prev(o[last])
        after = o[b + 1] if b < last else lane_next(o[0])
        out.append(jnp.where(low, before, after))
    return out


def around(o, halo, colour):
    xlo, xhi, ylo, yhi = halo
    zo = z_other(o, colour)
    out = []
    for b, a in enumerate(o):
        out.append(
            (
                jnp.concatenate([xlo[b], a[:-1]], axis=0),
                jnp.concatenate([a[1:], xhi[b]], axis=0),
                row_prev(a, ylo[b]),
                row_next(a, yhi[b]),
                a,
                zo[b],
            )
        )
    return out


def split_even(zero, one):
    even = even_cells(zero.shape)
    return jnp.where(even, zero, one), jnp.where(even, one, zero)


def pair_rows(a):
    rows = a.shape[1] // 2
    a = a.reshape(a.shape[0] // 2, 2, a.shape[1], LANES)
    a = a[:, 0] + a[:, 1]
    pick = iota((a.shape[0], rows, LANES), 1)
    out = a[:, 0:1] + a[:, 1:2]
    out = jnp.broadcast_to(out, pick.shape)
    for j in range(1, rows):
        out = jnp.where(pick == j, a[:, 2 * j : 2 * j + 1] + a[:, 2 * j + 1 : 2 * j + 2], out)
    return out * 0.125


def double_rows(a):
    x, rows, _ = a.shape
    pick = iota((x, 2 * rows, LANES), 1) // 2
    out = jnp.broadcast_to(a[:, 0:1], pick.shape)
    for j in range(1, rows):
        out = jnp.where(pick == j, a[:, j : j + 1], out)
    return jnp.concatenate([out[i // 2 : i // 2 + 1] for i in range(2 * x)], axis=0)


def three(x):
    high = x.astype(jnp.bfloat16)
    rest = x - high.astype(F32)
    middle = rest.astype(jnp.bfloat16)
    low = (rest - middle.astype(F32)).astype(jnp.bfloat16)
    return high, middle, low


def permute(x, matrix, side):
    parts = [
        lax.dot_general(part, matrix, (((1,), (side,)), ((), ())), preferred_element_type=F32)
        for part in three(x)
    ]
    return (parts[0] + parts[1]) + parts[2]


def kernel(nx, ny, g_ref, c_ref, v_out, r_out, perm, k0, k1, k2, sx0, sy0, rx0, ry0, sx1, sy1, rx1, ry1,
           ga, gb, vc, cw, sem0, sem1, semx, semy):
    gx, gy = lax.axis_index("gx"), lax.axis_index("gy")
    has = (gx > 0, gx < nx - 1, gy > 0, gy < ny - 1)
    peer = ({"gx": gx - 1}, {"gx": gx + 1}, {"gy": gy - 1}, {"gy": gy + 1})
    bufs = ((sx0, sy0, rx0, ry0, sem0), (sx1, sy1, rx1, ry1, sem1))

    for rx, ry in ((rx0, ry0), (rx1, ry1)):
        for d in range(4):
            ref = (rx, ry)[d // 2]

            @pl.when(jnp.logical_not(has[d]))
            def _():
                ref[:, d % 2] = jnp.zeros((ref.shape[0],) + ref.shape[2:], F32)

    barrier = pltpu.get_barrier_semaphore()
    for s in range(1, nx):
        pl.semaphore_signal(barrier, inc=1, device_id={"gx": lax.rem(gx + s, nx)}, device_id_type=MESH)
    for s in range(1, ny):
        pl.semaphore_signal(barrier, inc=1, device_id={"gy": lax.rem(gy + s, ny)}, device_id_type=MESH)

    size_z = 4 * LANES
    row, col = iota((size_z, size_z), 0), iota((size_z, size_z), 1)
    perm[...] = (row == 4 * (col % LANES) + col // LANES).astype(F32).astype(jnp.bfloat16)

    def unpack(ref):
        flat = permute(ref[...].reshape(-1, size_z), perm[...], 0)
        quarters = [flat[:, q * LANES : (q + 1) * LANES].reshape(ref.shape[0], ref.shape[1], LANES) for q in range(4)]
        pairs = [split_even(quarters[2 * b], quarters[2 * b + 1]) for b in range(2)]
        return [pairs[b][0] for b in range(2)], [pairs[b][1] for b in range(2)]

    def pack(ref, red, black):
        quarters = []
        for b in range(2):
            quarters.extend(split_even(red[b], black[b]))
        flat = jnp.concatenate([q.reshape(-1, LANES) for q in quarters], axis=1)
        ref[...] = permute(flat, perm[...], 1).reshape(ref.shape)

    def coarsen(red, black):
        pair = [pair_rows(red[b] + black[b]) for b in range(len(red))]
        if len(pair) == 1:
            return pair[0]
        first, second = split_even(pair[0], pair[1])
        return [first], [second]

    def copy(level, ph, d, into=False):
        sx, sy, rx, ry, sem = bufs[level]
        send, recv = (sx, rx) if d < 2 else (sy, ry)
        lands = d if into else d + 1 - 2 * (d % 2)
        return pltpu.make_async_remote_copy(
            src_ref=send.at[ph, d % 2], dst_ref=recv.at[ph, lands % 2], send_sem=sem.at[0, ph, d],
            recv_sem=sem.at[1, ph, lands], device_id=peer[d], device_id_type=MESH)

    def start(level, ph, o):
        sx, sy = bufs[level][:2]
        for b, a in enumerate(o):
            sx[ph, 0, b] = a[:1]
            sx[ph, 1, b] = a[-1:]
            sy[ph, 0, b] = a[:, :1]
            sy[ph, 1, b] = a[:, -1:]
        for d in range(4):
            @pl.when(has[d])
            def _():
                copy(level, ph, d).start()

    def finish(level, ph):
        for d in range(4):
            @pl.when(has[d])
            def _():
                copy(level, ph, d, into=True).wait_recv()
                copy(level, ph, d).wait_send()
        rx, ry = bufs[level][2:4]
        groups = range(rx.shape[2])
        return [[ref[ph, side, b] for b in groups] for ref in (rx, ry) for side in range(2)]

    phase = [0, 0]

    def swap(level, o):
        ph = phase[level]
        phase[level] += 1
        start(level, ph, o)
        return finish(level, ph)

    def gather_copy(stage, s):
        if stage == 0:
            return pltpu.make_async_remote_copy(
                src_ref=ga.at[gx], dst_ref=ga.at[gx], send_sem=semx.at[0, s], recv_sem=semx.at[1, s],
                device_id={"gx": lax.rem(gx + s, nx)}, device_id_type=MESH)
        return pltpu.make_async_remote_copy(
            src_ref=gb.at[gy], dst_ref=gb.at[gy], send_sem=semy.at[0, s], recv_sem=semy.at[1, s],
            device_id={"gy": lax.rem(gy + s, ny)}, device_id_type=MESH)

    def gather(dens, source):
        ga[gx, 0] = dens
        ga[gx, 1] = source
        for s in range(1, nx):
            gather_copy(0, s).start()
        for s in range(1, nx):
            src = lax.rem(gx + nx - s, nx)
            pltpu.make_async_remote_copy(
                src_ref=ga.at[src], dst_ref=ga.at[src], send_sem=semx.at[0, s], recv_sem=semx.at[1, s],
                device_id={"gx": src}, device_id_type=MESH).wait_recv()
            gather_copy(0, s).wait_send()
        for i in range(nx):
            gb[gy, 0, 2 * i : 2 * i + 2] = ga[i, 0]
            gb[gy, 1, 2 * i : 2 * i + 2] = ga[i, 1]
        for s in range(1, ny):
            gather_copy(1, s).start()
        for s in range(1, ny):
            src = lax.rem(gy + ny - s, ny)
            pltpu.make_async_remote_copy(
                src_ref=gb.at[src], dst_ref=gb.at[src], send_sem=semy.at[0, s], recv_sem=semy.at[1, s],
                device_id={"gy": src}, device_id_type=MESH).wait_recv()
            gather_copy(1, s).wait_send()

    def setup(kref, own, other, halo, colour, scale):
        for b, near in enumerate(around(other, halo, colour)):
            total = None
            for f in range(6):
                face = (scale * 0.5) * (own[b] + near[f])
                kref[colour, b, f] = face
                total = face if total is None else total + face
            kref[colour, b, 6] = total
            kref[colour, b, 7] = 1.0 / total

    def weigh(kref, o, halo, colour):
        out = []
        for b, near in enumerate(around(o, halo, colour)):
            total = kref[colour, b, 0] * near[0]
            for f in range(1, 6):
                total = total + kref[colour, b, f] * near[f]
            out.append(total)
        return out

    def update(kref, g, o, halo, colour):
        n = weigh(kref, o, halo, colour)
        return [(g[b] + n[b]) * kref[colour, b, 7] for b in range(len(n))]

    def remainder(kref, g, v, o, halo, colour):
        n = weigh(kref, o, halo, colour)
        return [g[b] - (kref[colour, b, 6] * v[b] - n[b]) for b in range(len(n))]

    def smooth(level, kref, g, v, sweeps):
        zero = v is None
        red, black = (None, None) if zero else v
        for sweep in range(sweeps):
            if zero and sweep == 0:
                red = [g[0][b] * kref[0, b, 7] for b in range(len(g[0]))]
            else:
                red = update(kref, g[0], black, swap(level, black), 0)
            red_halo = swap(level, red)
            black = update(kref, g[1], red, red_halo, 1)
        return red, black, red_halo

    def residual(level, kref, g, v):
        red, black, red_halo = v
        left = remainder(kref, g[1], black, red, red_halo, 1)
        return remainder(kref, g[0], red, black, swap(level, black), 0), left

    pl.semaphore_wait(barrier, nx - 1 + ny - 1)

    dens = unpack(c_ref)
    for c in range(2):
        start(0, c, dens[c])
    dens_one = coarsen(*dens)
    for c in range(2):
        start(1, c, dens_one[c])
    dens_two = coarsen(*dens_one)
    source = unpack(g_ref)
    for level, kref, d, scale in ((0, k0, dens, 1.0), (1, k1, dens_one, 0.25)):
        halos = [finish(level, c) for c in range(2)]
        phase[level] = 2
        for c in range(2):
            setup(kref, d[c], d[1 - c], halos[1 - c], c, scale)

    fine = smooth(0, k0, source, None, SWEEPS)
    source_one = coarsen(*residual(0, k0, source, fine))
    middle = smooth(1, k1, source_one, None, SWEEPS)
    source_two = coarsen(*residual(1, k1, source_one, middle))

    gather(dens_two, source_two)
    for j in range(ny):
        cw[0, :, 2 * j : 2 * j + 2] = gb[j, 0]
        cw[1, :, 2 * j : 2 * j + 2] = gb[j, 1]

    def sides(a):
        plane = jnp.zeros_like(a[:1])
        line = jnp.zeros_like(a[:, :1])
        return (
            jnp.concatenate([plane, a[:-1]], axis=0), jnp.concatenate([a[1:], plane], axis=0),
            row_prev(a, line), row_next(a, line), lane_prev(a), lane_next(a))

    centre = cw[0]
    total = None
    for f, near in enumerate(sides(centre)):
        face = 0.03125 * (centre + near)
        k2[f] = face
        total = face if total is None else total + face
    k2[6] = 1.0 / total
    shape = centre.shape
    red_two = (iota(shape, 0) + iota(shape, 1) + iota(shape, 2)) % 2 == 0
    cw[0] = jnp.zeros(shape, F32)

    def half(red):
        field = cw[0]
        total = cw[1]
        for f, near in enumerate(sides(field)):
            total = total + k2[f] * near
        total = total * k2[6]
        cw[0] = jnp.where(red_two, total, field) if red else jnp.where(red_two, field, total)

    def sweep(i, carry):
        half(True)
        half(False)
        return carry

    lax.fori_loop(0, COARSE_SWEEPS, sweep, 0)
    field = cw[0]
    for j in range(ny):
        vc[j] = field[:, 2 * j : 2 * j + 2]
    add = double_rows(vc[gy, pl.ds(2 * gx, 2)])
    middle = smooth(1, k1, source_one, [[v[0] + add] for v in middle[:2]], SWEEPS)
    adds = [double_rows(a) for a in split_even(middle[0][0], middle[1][0])]
    fine = smooth(0, k0, source, [[v[b] + adds[b] for b in range(2)] for v in fine[:2]], SWEEPS)
    pack(v_out, fine[0], fine[1])
    left = residual(0, k0, source, fine)
    pack(r_out, left[0], left[1])


def solution(mesh):
    nx, ny = mesh.shape["gx"], mesh.shape["gy"]

    def shards(right_side, inverse_density):
        x, y, z = right_side.shape
        x1, y1 = x // 2, y // 2
        p0, p1 = 4 * SWEEPS + 3, 4 * SWEEPS + 2
        halo0 = [pltpu.VMEM((p0, 2, 2, 1, y, LANES), F32), pltpu.VMEM((p0, 2, 2, x, 1, LANES), F32)]
        halo1 = [pltpu.VMEM((p1, 2, 1, 1, y1, LANES), F32), pltpu.VMEM((p1, 2, 1, x1, 1, LANES), F32)]
        out = jax.ShapeDtypeStruct(right_side.shape, F32)
        return pl.pallas_call(
            functools.partial(kernel, nx, ny),
            out_shape=(out, out),
            in_specs=[pl.BlockSpec(memory_space=pltpu.VMEM)] * 2,
            out_specs=(pl.BlockSpec(memory_space=pltpu.VMEM),) * 2,
            scratch_shapes=[
                pltpu.VMEM((z, z), jnp.bfloat16),
                pltpu.VMEM((2, 2, 8, x, y, LANES), F32),
                pltpu.VMEM((2, 1, 8, x1, y1, LANES), F32),
                pltpu.VMEM((7, nx * x // 4, ny * y // 4, LANES), F32),
                *halo0, *halo0, *halo1, *halo1,
                pltpu.VMEM((nx, 2, x // 4, y // 4, LANES), F32),
                pltpu.VMEM((ny, 2, nx * x // 4, y // 4, LANES), F32),
                pltpu.VMEM((ny, nx * x // 4, y // 4, LANES), F32),
                pltpu.VMEM((2, nx * x // 4, ny * y // 4, LANES), F32),
                pltpu.SemaphoreType.DMA((2, p0, 4)),
                pltpu.SemaphoreType.DMA((2, p1, 4)),
                pltpu.SemaphoreType.DMA((2, nx)),
                pltpu.SemaphoreType.DMA((2, ny)),
            ],
            compiler_params=pltpu.CompilerParams(
                collective_id=0, has_side_effects=True, vmem_limit_bytes=48 * 1024 * 1024
            ),
        )(right_side, inverse_density)

    spec = P("gx", "gy", None)
    return jax.shard_map(shards, mesh=mesh, in_specs=(spec, spec), out_specs=(spec, spec), check_vma=False)
```

```python
import functools

import jax
import jax.numpy as jnp
from jax import lax
from jax.experimental import pallas as pl
from jax.experimental.pallas import tpu as pltpu
from jax.sharding import PartitionSpec as P

SWEEPS = 2
COARSE_SWEEPS = 8
MESH = pl.DeviceIdType.MESH
LANES = 128
F32 = jnp.float32


def iota(shape, dim):
    return lax.broadcasted_iota(jnp.int32, shape, dim)


def lane_prev(a):
    return jnp.where(iota(a.shape, 2) == 0, 0.0, pltpu.roll(a, 1, 2))


def lane_next(a):
    return jnp.where(iota(a.shape, 2) == LANES - 1, 0.0, pltpu.roll(a, LANES - 1, 2))


def row_prev(a, halo):
    return jnp.where(iota(a.shape, 1) == 0, halo, pltpu.roll(a, 1, 1)) if a.shape[1] % 8 == 0 else jnp.concatenate(
        [halo, a[:, :-1]], axis=1
    )


def row_next(a, halo):
    rows = a.shape[1]
    return jnp.where(iota(a.shape, 1) == rows - 1, halo, pltpu.roll(a, rows - 1, 1)) if rows % 8 == 0 else jnp.concatenate(
        [a[:, 1:], halo], axis=1
    )


def even_cells(shape):
    return (iota(shape, 0) + iota(shape, 1)) % 2 == 0


REGION_Y = 16


def z_other(o, colour, first):
    shape = o[0].shape
    even = (iota(shape, 0) + iota(shape, 1)) % 2 == first % 2
    low = even if colour == 0 else jnp.logical_not(even)
    last = len(o) - 1
    out = []
    for b in range(last + 1):
        before = o[b - 1] if b > 0 else lane_prev(o[last])
        after = o[b + 1] if b < last else lane_next(o[0])
        out.append(jnp.where(low, before, after))
    return out


def around(ref, colour, x0, x1):
    other = 1 - colour
    groups = range(ref.shape[1])
    mid = [ref[other, b, x0:x1] for b in groups]
    zo = z_other(mid, colour, x0)
    return [
        (
            ref[other, b, x0 - 1 : x1 - 1],
            ref[other, b, x0 + 1 : x1 + 1],
            pltpu.roll(mid[b], 1, 1),
            pltpu.roll(mid[b], REGION_Y - 1, 1),
            mid[b],
            zo[b],
        )
        for b in groups
    ]


def split_even(zero, one):
    even = even_cells(zero.shape)
    return jnp.where(even, zero, one), jnp.where(even, one, zero)


def pair_rows(a):
    rows = a.shape[1] // 2
    a = a.reshape(a.shape[0] // 2, 2, a.shape[1], LANES)
    a = a[:, 0] + a[:, 1]
    pick = iota((a.shape[0], rows, LANES), 1)
    out = a[:, 0:1] + a[:, 1:2]
    out = jnp.broadcast_to(out, pick.shape)
    for j in range(1, rows):
        out = jnp.where(pick == j, a[:, 2 * j : 2 * j + 1] + a[:, 2 * j + 1 : 2 * j + 2], out)
    return out * 0.125


def double_rows(a):
    x, rows, _ = a.shape
    pick = iota((x, 2 * rows, LANES), 1) // 2
    out = jnp.broadcast_to(a[:, 0:1], pick.shape)
    for j in range(1, rows):
        out = jnp.where(pick == j, a[:, j : j + 1], out)
    return jnp.concatenate([out[i // 2 : i // 2 + 1] for i in range(2 * x)], axis=0)


def three(x):
    high = x.astype(jnp.bfloat16)
    rest = x - high.astype(F32)
    middle = rest.astype(jnp.bfloat16)
    low = (rest - middle.astype(F32)).astype(jnp.bfloat16)
    return high, middle, low


def permute(x, matrix, side):
    parts = [
        lax.dot_general(part, matrix, (((1,), (side,)), ((), ())), preferred_element_type=F32)
        for part in three(x)
    ]
    return (parts[0] + parts[1]) + parts[2]


def kernel(nx, ny, g_ref, c_ref, v_out, r_out, perm, k0, d0, v0, g0, k1, d1, v1, g1, k2,
           sx0, sy0, sc0, rx0, ry0, rc0, sx1, sy1, sc1, rx1, ry1, rc1, ga, gb, vc, cw, sem0, sem1, semx, semy):
    gx, gy = lax.axis_index("gx"), lax.axis_index("gy")
    send = ((sx0, sy0, sc0), (sx1, sy1, sc1))
    recv = ((rx0, ry0, rc0), (rx1, ry1, rc1))
    sems = (sem0, sem1)
    size_x, size_y = g_ref.shape[:2]
    own_x, own_y, ring = (size_x, size_x // 2), (size_y, size_y // 2), (2, 4)
    near_x = {-1: gx > 0, 0: None, 1: gx < nx - 1}
    near_y = {-1: gy > 0, 0: None, 1: gy < ny - 1}

    ways = []
    for dx, dy in ((-1, 0), (1, 0), (0, -1), (0, 1), (-1, -1), (-1, 1), (1, -1), (1, 1)):
        kind = 2 if dx and dy else (0 if dx else 1)
        side = {0: (dx + 1) // 2, 1: (dy + 1) // 2, 2: (dx + 1) + (dy + 1) // 2}[kind]
        if dx and dy:
            has = jnp.logical_and(near_x[dx], near_y[dy])
        else:
            has = near_x[dx] if dx else near_y[dy]
        target = {}
        if dx:
            target["gx"] = gx + dx
        if dy:
            target["gy"] = gy + dy
        ways.append((dx, dy, kind, side, has, target))
    back = (1, 0, 3, 2, 7, 6, 5, 4)

    for level in range(2):
        for dx, dy, kind, side, has, target in ways:
            @pl.when(jnp.logical_not(has))
            def _():
                ref = recv[level][kind]
                ref[:, side] = jnp.zeros((ref.shape[0],) + ref.shape[2:], F32)

    for ref in (d0, v0, g0, d1, v1, g1):
        ref[...] = jnp.zeros(ref.shape, F32)
    for c in range(2):
        k1[c, 0, 7] = jnp.zeros(k1.shape[3:], F32)

    barrier = pltpu.get_barrier_semaphore()
    for s in range(1, nx):
        pl.semaphore_signal(barrier, inc=1, device_id={"gx": lax.rem(gx + s, nx)}, device_id_type=MESH)
    for s in range(1, ny):
        pl.semaphore_signal(barrier, inc=1, device_id={"gy": lax.rem(gy + s, ny)}, device_id_type=MESH)
    for dx, dy, kind, side, has, target in ways[4:]:
        @pl.when(has)
        def _():
            pl.semaphore_signal(barrier, inc=1, device_id=target, device_id_type=MESH)

    size_z = 4 * LANES
    row, col = iota((size_z, size_z), 0), iota((size_z, size_z), 1)
    perm[...] = (row == 4 * (col % LANES) + col // LANES).astype(F32).astype(jnp.bfloat16)

    def unpack(ref):
        flat = permute(ref[...].reshape(-1, size_z), perm[...], 0)
        quarters = [flat[:, q * LANES : (q + 1) * LANES].reshape(ref.shape[0], ref.shape[1], LANES) for q in range(4)]
        pairs = [split_even(quarters[2 * b], quarters[2 * b + 1]) for b in range(2)]
        return [pairs[b][0] for b in range(2)], [pairs[b][1] for b in range(2)]

    def pack(ref, red, black):
        quarters = []
        for b in range(2):
            quarters.extend(split_even(red[b], black[b]))
        flat = jnp.concatenate([q.reshape(-1, LANES) for q in quarters], axis=1)
        ref[...] = permute(flat, perm[...], 1).reshape(ref.shape)

    def coarsen(red, black):
        pair = [pair_rows(red[b] + black[b]) for b in range(len(red))]
        if len(pair) == 1:
            return pair[0]
        first, second = split_even(pair[0], pair[1])
        return [first], [second]

    def copy(level, ph, d, count, into=False):
        dx, dy, kind, side, has, target = ways[d]
        lands = d if into else back[d]
        sem = sems[level]
        return pltpu.make_async_remote_copy(
            src_ref=send[level][kind].at[ph, side, pl.ds(0, count)],
            dst_ref=recv[level][kind].at[ph, ways[lands][3], pl.ds(0, count)],
            send_sem=sem.at[0, ph, d], recv_sem=sem.at[1, ph, lands], device_id=target, device_id_type=MESH)

    def span(step, own, width, edge):
        if step == 0:
            return slice(width, width + own)
        if edge == "send":
            return slice(width, 2 * width) if step < 0 else slice(own, own + width)
        return slice(0, width) if step < 0 else slice(width + own, 2 * width + own)

    def start(level, ph, fields):
        x, y, h = own_x[level], own_y[level], ring[level]
        for dx, dy, kind, side, has, target in ways:
            for f, ref in enumerate(fields):
                send[level][kind][ph, side, f] = ref[span(dx, x, h, "send"), span(dy, y, h, "send"), :]
        for d, way in enumerate(ways):
            @pl.when(way[4])
            def _():
                copy(level, ph, d, len(fields)).start()

    def finish(level, ph, fields):
        x, y, h = own_x[level], own_y[level], ring[level]
        for d, way in enumerate(ways):
            @pl.when(way[4])
            def _():
                copy(level, ph, d, len(fields), into=True).wait_recv()
                copy(level, ph, d, len(fields)).wait_send()
        for dx, dy, kind, side, has, target in ways:
            for f, ref in enumerate(fields):
                ref[span(dx, x, h, ""), span(dy, y, h, ""), :] = recv[level][kind][ph, side, f]

    def swap(level, ph, fields):
        start(level, ph, fields)
        finish(level, ph, fields)

    def both(ref):
        return [ref.at[c, b] for c in range(2) for b in range(ref.shape[1])]

    def black(ref):
        return [ref.at[1, b] for b in range(ref.shape[1])]

    def own(level, a):
        x, y, h = own_x[level], own_y[level], ring[level]
        return a[h : h + x, h : h + y]

    def place(level, ref, fields, add=False):
        x, y, h = own_x[level], own_y[level], ring[level]
        for c in range(2):
            for b, a in enumerate(fields[c]):
                if add:
                    a = a + ref[c, b, h : h + x, h : h + y]
                ref[c, b, h : h + x, h : h + y] = a

    def gather_copy(stage, s):
        if stage == 0:
            return pltpu.make_async_remote_copy(
                src_ref=ga.at[gx], dst_ref=ga.at[gx], send_sem=semx.at[0, s], recv_sem=semx.at[1, s],
                device_id={"gx": lax.rem(gx + s, nx)}, device_id_type=MESH)
        return pltpu.make_async_remote_copy(
            src_ref=gb.at[gy], dst_ref=gb.at[gy], send_sem=semy.at[0, s], recv_sem=semy.at[1, s],
            device_id={"gy": lax.rem(gy + s, ny)}, device_id_type=MESH)

    def gather(dens, source):
        ga[gx, 0] = dens
        ga[gx, 1] = source
        for s in range(1, nx):
            gather_copy(0, s).start()
        for s in range(1, nx):
            src = lax.rem(gx + nx - s, nx)
            pltpu.make_async_remote_copy(
                src_ref=ga.at[src], dst_ref=ga.at[src], send_sem=semx.at[0, s], recv_sem=semx.at[1, s],
                device_id={"gx": src}, device_id_type=MESH).wait_recv()
            gather_copy(0, s).wait_send()
        for i in range(nx):
            gb[gy, 0, 2 * i : 2 * i + 2] = ga[i, 0]
            gb[gy, 1, 2 * i : 2 * i + 2] = ga[i, 1]
        for s in range(1, ny):
            gather_copy(1, s).start()
        for s in range(1, ny):
            src = lax.rem(gy + ny - s, ny)
            pltpu.make_async_remote_copy(
                src_ref=gb.at[src], dst_ref=gb.at[src], send_sem=semy.at[0, s], recv_sem=semy.at[1, s],
                device_id={"gy": src}, device_id_type=MESH).wait_recv()
            gather_copy(1, s).wait_send()

    def setup(kref, dens, colour, scale):
        x0, x1 = 1, dens.shape[2] - 1
        for b, near in enumerate(around(dens, colour, x0, x1)):
            here = dens[colour, b, x0:x1]
            total = None
            for f in range(6):
                face = (scale * 0.5) * (here + near[f])
                kref[colour, b, f, x0:x1] = face
                total = face if total is None else total + face
            kref[colour, b, 6, x0:x1] = total
            kref[colour, b, 7, x0:x1] = jnp.where(here > 0.0, 1.0 / total, 0.0)

    def weigh(kref, v, colour, x0, x1):
        out = []
        for b, near in enumerate(around(v, colour, x0, x1)):
            total = kref[colour, b, 0, x0:x1] * near[0]
            for f in range(1, 6):
                total = total + kref[colour, b, f, x0:x1] * near[f]
            out.append(total)
        return out

    def update(kref, g, v, colour, x0, x1):
        for b, n in enumerate(weigh(kref, v, colour, x0, x1)):
            v[colour, b, x0:x1] = (g[colour, b, x0:x1] + n) * kref[colour, b, 7, x0:x1]

    def first(kref, g, v, x0, x1):
        for b in range(v.shape[1]):
            v[0, b, x0:x1] = g[0, b, x0:x1] * kref[0, b, 7, x0:x1]

    def residual(level, kref, g, v):
        h = ring[level]
        x0, x1 = h, h + own_x[level]
        out = []
        for c in range(2):
            n = weigh(kref, v, c, x0, x1)
            out.append([
                (g[c, b, x0:x1] - (kref[c, b, 6, x0:x1] * v[c, b, x0:x1] - n[b]))[:, h : h + own_y[level]]
                for b in range(len(n))])
        return out

    beside_x = (gx > 0).astype(jnp.int32) + (gx < nx - 1).astype(jnp.int32)
    beside_y = (gy > 0).astype(jnp.int32) + (gy < ny - 1).astype(jnp.int32)
    pl.semaphore_wait(barrier, nx + ny - 2 + beside_x * beside_y)

    dens = unpack(c_ref)
    place(0, d0, dens)
    start(0, 0, both(d0))
    dens_one = coarsen(*dens)
    place(1, d1, dens_one)
    start(1, 0, both(d1))
    dens_two = coarsen(*dens_one)
    place(0, g0, unpack(g_ref))
    start(0, 1, both(g0))
    inverse = [k1.at[c, 0, 7] for c in range(2)]
    finish(1, 0, both(d1))
    for c in range(2):
        setup(k1, d1, c, 0.25)
    start(1, 1, inverse)
    finish(0, 0, both(d0))
    for c in range(2):
        setup(k0, d0, c, 1.0)
    finish(0, 1, both(g0))

    high = 2 + size_x
    first(k0, g0, v0, 1, high + 1)
    update(k0, g0, v0, 1, 2, high)
    for s in range(1, SWEEPS):
        swap(0, 1 + s, black(v0))
        update(k0, g0, v0, 0, 1, high + 1)
        update(k0, g0, v0, 1, 2, high)
    swap(0, 1 + SWEEPS, black(v0))
    place(1, g1, coarsen(*residual(0, k0, g0, v0)))

    start(1, 2, both(g1))
    finish(1, 1, inverse)
    finish(1, 2, both(g1))
    wide = v1.shape[2]
    first(k1, g1, v1, 0, wide)
    for s in range(1, 2 * SWEEPS):
        update(k1, g1, v1, s % 2, s, wide - s)
    start(1, 3, both(v1))
    source_two = coarsen(*residual(1, k1, g1, v1))

    gather(dens_two, source_two)
    for j in range(ny):
        cw[0, :, 2 * j : 2 * j + 2] = gb[j, 0]
        cw[1, :, 2 * j : 2 * j + 2] = gb[j, 1]

    def sides(a):
        plane = jnp.zeros_like(a[:1])
        line = jnp.zeros_like(a[:, :1])
        return (
            jnp.concatenate([plane, a[:-1]], axis=0), jnp.concatenate([a[1:], plane], axis=0),
            row_prev(a, line), row_next(a, line), lane_prev(a), lane_next(a))

    centre = cw[0]
    total = None
    for f, near in enumerate(sides(centre)):
        face = 0.03125 * (centre + near)
        k2[f] = face
        total = face if total is None else total + face
    k2[6] = 1.0 / total
    shape = centre.shape
    red_two = (iota(shape, 0) + iota(shape, 1) + iota(shape, 2)) % 2 == 0
    cw[0] = jnp.zeros(shape, F32)

    def half(red):
        field = cw[0]
        total = cw[1]
        for f, near in enumerate(sides(field)):
            total = total + k2[f] * near
        total = total * k2[6]
        cw[0] = jnp.where(red_two, total, field) if red else jnp.where(red_two, field, total)

    def sweep(i, carry):
        half(True)
        half(False)
        return carry

    lax.fori_loop(0, COARSE_SWEEPS, sweep, 0)
    field = cw[0]
    vc[...] = jnp.zeros(vc.shape, F32)
    for j in range(ny):
        vc[1 + j, 2 : 2 + 2 * nx] = field[:, 2 * j : 2 * j + 2]
    finish(1, 3, both(v1))
    for dy in range(3):
        add = double_rows(vc[gy + dy, pl.ds(2 * gx, 6)])
        for c in range(2):
            v1[c, 0, :, 4 * dy : 4 * dy + 4] = v1[c, 0, :, 4 * dy : 4 * dy + 4] + add
    for s in range(2 * SWEEPS):
        update(k1, g1, v1, s % 2, s + 1, wide - s - 1)

    adds = [double_rows(a) for a in split_even(own(1, v1[0, 0]), own(1, v1[1, 0]))]
    place(0, v0, [adds, adds], add=True)
    for s in range(SWEEPS):
        swap(0, 2 + SWEEPS + s, black(v0))
        update(k0, g0, v0, 0, 1, high + 1)
        update(k0, g0, v0, 1, 2, high)
    start(0, 2 + 2 * SWEEPS, black(v0))
    pack(v_out, *[[own(0, v0[c, b]) for b in range(2)] for c in range(2)])
    finish(0, 2 + 2 * SWEEPS, black(v0))
    pack(r_out, *residual(0, k0, g0, v0))


def solution(mesh):
    nx, ny = mesh.shape["gx"], mesh.shape["gy"]

    def shards(right_side, inverse_density):
        x, y, z = right_side.shape
        p0, p1 = 3 + 2 * SWEEPS, 4

        def halo(phases, fields, own_x, own_y, ring):
            return [
                pltpu.VMEM((phases, 2, fields, ring, own_y, LANES), F32),
                pltpu.VMEM((phases, 2, fields, own_x, ring, LANES), F32),
                pltpu.VMEM((phases, 4, fields, ring, ring, LANES), F32),
            ]

        def level(groups, rows):
            field = pltpu.VMEM((2, groups, rows, REGION_Y, LANES), F32)
            return [pltpu.VMEM((2, groups, 8, rows, REGION_Y, LANES), F32), field, field, field]

        halo0 = halo(p0, 4, x, y, 2)
        halo1 = halo(p1, 2, x // 2, y // 2, 4)
        out = jax.ShapeDtypeStruct(right_side.shape, F32)
        return pl.pallas_call(
            functools.partial(kernel, nx, ny),
            out_shape=(out, out),
            in_specs=[pl.BlockSpec(memory_space=pltpu.VMEM)] * 2,
            out_specs=(pl.BlockSpec(memory_space=pltpu.VMEM),) * 2,
            scratch_shapes=[
                pltpu.VMEM((z, z), jnp.bfloat16),
                *level(2, x + 4),
                *level(1, x // 2 + 8),
                pltpu.VMEM((7, nx * x // 4, ny * y // 4, LANES), F32),
                *halo0, *halo0, *halo1, *halo1,
                pltpu.VMEM((nx, 2, x // 4, y // 4, LANES), F32),
                pltpu.VMEM((ny, 2, nx * x // 4, y // 4, LANES), F32),
                pltpu.VMEM((ny + 2, nx * x // 4 + 4, y // 4, LANES), F32),
                pltpu.VMEM((2, nx * x // 4, ny * y // 4, LANES), F32),
                pltpu.SemaphoreType.DMA((2, p0, 8)),
                pltpu.SemaphoreType.DMA((2, p1, 8)),
                pltpu.SemaphoreType.DMA((2, nx)),
                pltpu.SemaphoreType.DMA((2, ny)),
            ],
            compiler_params=pltpu.CompilerParams(
                collective_id=0, has_side_effects=True, vmem_limit_bytes=48 * 1024 * 1024
            ),
        )(right_side, inverse_density)

    spec = P("gx", "gy", None)
    return jax.shard_map(shards, mesh=mesh, in_specs=(spec, spec), out_specs=(spec, spec), check_vma=False)
```

```python
import functools

import jax
import jax.numpy as jnp
from jax import lax
from jax.experimental import pallas as pl
from jax.experimental.pallas import tpu as pltpu
from jax.sharding import PartitionSpec as P

SWEEPS = 2
COARSE_SWEEPS = 8
MESH = pl.DeviceIdType.MESH
LANES = 128
F32 = jnp.float32


def iota(shape, dim):
    return lax.broadcasted_iota(jnp.int32, shape, dim)


def lane_prev(a):
    return jnp.where(iota(a.shape, 2) == 0, 0.0, pltpu.roll(a, 1, 2))


def lane_next(a):
    return jnp.where(iota(a.shape, 2) == LANES - 1, 0.0, pltpu.roll(a, LANES - 1, 2))


def row_prev(a, halo):
    return jnp.where(iota(a.shape, 1) == 0, halo, pltpu.roll(a, 1, 1)) if a.shape[1] % 8 == 0 else jnp.concatenate(
        [halo, a[:, :-1]], axis=1
    )


def row_next(a, halo):
    rows = a.shape[1]
    return jnp.where(iota(a.shape, 1) == rows - 1, halo, pltpu.roll(a, rows - 1, 1)) if rows % 8 == 0 else jnp.concatenate(
        [a[:, 1:], halo], axis=1
    )


def even_cells(shape):
    return (iota(shape, 0) + iota(shape, 1)) % 2 == 0


REGION_Y = 16


def z_other(o, colour, first):
    shape = o[0].shape
    even = (iota(shape, 0) + iota(shape, 1)) % 2 == first % 2
    low = even if colour == 0 else jnp.logical_not(even)
    last = len(o) - 1
    out = []
    for b in range(last + 1):
        before = o[b - 1] if b > 0 else lane_prev(o[last])
        after = o[b + 1] if b < last else lane_next(o[0])
        out.append(jnp.where(low, before, after))
    return out


def around(ref, colour, x0, x1):
    other = 1 - colour
    groups = range(ref.shape[1])
    mid = [ref[other, b, x0:x1] for b in groups]
    zo = z_other(mid, colour, x0)
    return [
        (
            ref[other, b, x0 - 1 : x1 - 1],
            ref[other, b, x0 + 1 : x1 + 1],
            pltpu.roll(mid[b], 1, 1),
            pltpu.roll(mid[b], REGION_Y - 1, 1),
            mid[b],
            zo[b],
        )
        for b in groups
    ]


def split_even(zero, one):
    even = even_cells(zero.shape)
    return jnp.where(even, zero, one), jnp.where(even, one, zero)


def pair_rows(a):
    rows = a.shape[1] // 2
    a = a.reshape(a.shape[0] // 2, 2, a.shape[1], LANES)
    a = a[:, 0] + a[:, 1]
    pick = iota((a.shape[0], rows, LANES), 1)
    out = a[:, 0:1] + a[:, 1:2]
    out = jnp.broadcast_to(out, pick.shape)
    for j in range(1, rows):
        out = jnp.where(pick == j, a[:, 2 * j : 2 * j + 1] + a[:, 2 * j + 1 : 2 * j + 2], out)
    return out * 0.125


def double_rows(a):
    x, rows, _ = a.shape
    pick = iota((x, 2 * rows, LANES), 1) // 2
    out = jnp.broadcast_to(a[:, 0:1], pick.shape)
    for j in range(1, rows):
        out = jnp.where(pick == j, a[:, j : j + 1], out)
    return jnp.concatenate([out[i // 2 : i // 2 + 1] for i in range(2 * x)], axis=0)


def three(x):
    high = x.astype(jnp.bfloat16)
    rest = x - high.astype(F32)
    middle = rest.astype(jnp.bfloat16)
    low = (rest - middle.astype(F32)).astype(jnp.bfloat16)
    return high, middle, low


def permute(x, matrix, side):
    parts = [
        lax.dot_general(part, matrix, (((1,), (side,)), ((), ())), preferred_element_type=F32)
        for part in three(x)
    ]
    return (parts[0] + parts[1]) + parts[2]


def kernel(nx, ny, g_ref, c_ref, v_out, r_out, perm, k0, d0, v0, g0, k1, d1, v1, g1, k2,
           sx0, sy0, sc0, rx0, ry0, rc0, sx1, sy1, sc1, rx1, ry1, rc1, ga, gb, vc, cw, held, sem0, sem1, semx, semy, held_sem):
    gx, gy = lax.axis_index("gx"), lax.axis_index("gy")
    send = ((sx0, sy0, sc0), (sx1, sy1, sc1))
    recv = ((rx0, ry0, rc0), (rx1, ry1, rc1))
    sems = (sem0, sem1)
    size_x, size_y = g_ref.shape[:2]
    own_x, own_y, ring = (size_x, size_x // 2), (size_y, size_y // 2), (2, 4)
    near_x = {-1: gx > 0, 0: None, 1: gx < nx - 1}
    near_y = {-1: gy > 0, 0: None, 1: gy < ny - 1}

    ways = []
    for dx, dy in ((-1, 0), (1, 0), (0, -1), (0, 1), (-1, -1), (-1, 1), (1, -1), (1, 1)):
        kind = 2 if dx and dy else (0 if dx else 1)
        side = {0: (dx + 1) // 2, 1: (dy + 1) // 2, 2: (dx + 1) + (dy + 1) // 2}[kind]
        if dx and dy:
            has = jnp.logical_and(near_x[dx], near_y[dy])
        else:
            has = near_x[dx] if dx else near_y[dy]
        target = {}
        if dx:
            target["gx"] = gx + dx
        if dy:
            target["gy"] = gy + dy
        ways.append((dx, dy, kind, side, has, target))
    back = (1, 0, 3, 2, 7, 6, 5, 4)

    loads = [
        pltpu.make_async_copy(ref, held.at[n], held_sem.at[n]) for n, ref in enumerate((c_ref, g_ref))
    ]
    for load in loads:
        load.start()

    barrier = pltpu.get_barrier_semaphore()
    for s in range(1, nx):
        pl.semaphore_signal(barrier, inc=1, device_id={"gx": lax.rem(gx + s, nx)}, device_id_type=MESH)
    for s in range(1, ny):
        pl.semaphore_signal(barrier, inc=1, device_id={"gy": lax.rem(gy + s, ny)}, device_id_type=MESH)
    for dx, dy, kind, side, has, target in ways[4:]:
        @pl.when(has)
        def _():
            pl.semaphore_signal(barrier, inc=1, device_id=target, device_id_type=MESH)

    for level in range(2):
        for dx, dy, kind, side, has, target in ways:
            @pl.when(jnp.logical_not(has))
            def _():
                ref = recv[level][kind]
                ref[:, side] = jnp.zeros((ref.shape[0],) + ref.shape[2:], F32)

    for ref in (d0, v0, g0, d1, v1, g1):
        ref[...] = jnp.zeros(ref.shape, F32)
    for c in range(2):
        k1[c, 0, 7] = jnp.zeros(k1.shape[3:], F32)

    size_z = 4 * LANES
    row, col = iota((size_z, size_z), 0), iota((size_z, size_z), 1)
    perm[...] = (row == 4 * (col % LANES) + col // LANES).astype(F32).astype(jnp.bfloat16)

    def unpack(ref):
        flat = permute(ref[...].reshape(-1, size_z), perm[...], 0)
        quarters = [flat[:, q * LANES : (q + 1) * LANES].reshape(ref.shape[0], ref.shape[1], LANES) for q in range(4)]
        pairs = [split_even(quarters[2 * b], quarters[2 * b + 1]) for b in range(2)]
        return [pairs[b][0] for b in range(2)], [pairs[b][1] for b in range(2)]

    def pack(ref, red, black):
        quarters = []
        for b in range(2):
            quarters.extend(split_even(red[b], black[b]))
        flat = jnp.concatenate([q.reshape(-1, LANES) for q in quarters], axis=1)
        ref[...] = permute(flat, perm[...], 1).reshape(ref.shape)

    def coarsen(red, black):
        pair = [pair_rows(red[b] + black[b]) for b in range(len(red))]
        if len(pair) == 1:
            return pair[0]
        first, second = split_even(pair[0], pair[1])
        return [first], [second]

    def copy(level, ph, d, count, into=False):
        dx, dy, kind, side, has, target = ways[d]
        lands = d if into else back[d]
        sem = sems[level]
        return pltpu.make_async_remote_copy(
            src_ref=send[level][kind].at[ph, side, pl.ds(0, count)],
            dst_ref=recv[level][kind].at[ph, ways[lands][3], pl.ds(0, count)],
            send_sem=sem.at[0, ph, d], recv_sem=sem.at[1, ph, lands], device_id=target, device_id_type=MESH)

    def span(step, own, width, edge):
        if step == 0:
            return slice(width, width + own)
        if edge == "send":
            return slice(width, 2 * width) if step < 0 else slice(own, own + width)
        return slice(0, width) if step < 0 else slice(width + own, 2 * width + own)

    def start(level, ph, fields, count=8):
        x, y, h = own_x[level], own_y[level], ring[level]
        for dx, dy, kind, side, has, target in ways[:count]:
            for f, ref in enumerate(fields):
                send[level][kind][ph, side, f] = ref[span(dx, x, h, "send"), span(dy, y, h, "send"), :]
        for d, way in enumerate(ways[:count]):
            @pl.when(way[4])
            def _():
                copy(level, ph, d, len(fields)).start()

    def finish(level, ph, fields, count=8):
        x, y, h = own_x[level], own_y[level], ring[level]
        for d, way in enumerate(ways[:count]):
            @pl.when(way[4])
            def _():
                copy(level, ph, d, len(fields), into=True).wait_recv()
                copy(level, ph, d, len(fields)).wait_send()
        for dx, dy, kind, side, has, target in ways[:count]:
            for f, ref in enumerate(fields):
                ref[span(dx, x, h, ""), span(dy, y, h, ""), :] = recv[level][kind][ph, side, f]

    def swap(level, ph, fields, count=8):
        start(level, ph, fields, count)
        finish(level, ph, fields, count)

    def both(ref):
        return [ref.at[c, b] for c in range(2) for b in range(ref.shape[1])]

    def black(ref):
        return [ref.at[1, b] for b in range(ref.shape[1])]

    def own(level, a):
        x, y, h = own_x[level], own_y[level], ring[level]
        return a[h : h + x, h : h + y]

    def place(level, ref, fields, add=False):
        x, y, h = own_x[level], own_y[level], ring[level]
        for c in range(2):
            for b, a in enumerate(fields[c]):
                if add:
                    a = a + ref[c, b, h : h + x, h : h + y]
                ref[c, b, h : h + x, h : h + y] = a

    def gather_copy(stage, s):
        if stage == 0:
            return pltpu.make_async_remote_copy(
                src_ref=ga.at[gx], dst_ref=ga.at[gx], send_sem=semx.at[0, s], recv_sem=semx.at[1, s],
                device_id={"gx": lax.rem(gx + s, nx)}, device_id_type=MESH)
        return pltpu.make_async_remote_copy(
            src_ref=gb.at[gy], dst_ref=gb.at[gy], send_sem=semy.at[0, s], recv_sem=semy.at[1, s],
            device_id={"gy": lax.rem(gy + s, ny)}, device_id_type=MESH)

    def gather(dens, source):
        ga[gx, 0] = dens
        ga[gx, 1] = source
        for s in range(1, nx):
            gather_copy(0, s).start()
        for s in range(1, nx):
            src = lax.rem(gx + nx - s, nx)
            pltpu.make_async_remote_copy(
                src_ref=ga.at[src], dst_ref=ga.at[src], send_sem=semx.at[0, s], recv_sem=semx.at[1, s],
                device_id={"gx": src}, device_id_type=MESH).wait_recv()
            gather_copy(0, s).wait_send()
        for i in range(nx):
            gb[gy, 0, 2 * i : 2 * i + 2] = ga[i, 0]
            gb[gy, 1, 2 * i : 2 * i + 2] = ga[i, 1]
        for s in range(1, ny):
            gather_copy(1, s).start()
        for s in range(1, ny):
            src = lax.rem(gy + ny - s, ny)
            pltpu.make_async_remote_copy(
                src_ref=gb.at[src], dst_ref=gb.at[src], send_sem=semy.at[0, s], recv_sem=semy.at[1, s],
                device_id={"gy": src}, device_id_type=MESH).wait_recv()
            gather_copy(1, s).wait_send()

    def setup(kref, dens, colour, scale):
        x0, x1 = 1, dens.shape[2] - 1
        for b, near in enumerate(around(dens, colour, x0, x1)):
            here = dens[colour, b, x0:x1]
            total = None
            for f in range(6):
                face = (scale * 0.5) * (here + near[f])
                kref[colour, b, f, x0:x1] = face
                total = face if total is None else total + face
            kref[colour, b, 6, x0:x1] = total
            kref[colour, b, 7, x0:x1] = jnp.where(here > 0.0, 1.0 / total, 0.0)

    def weigh(kref, v, colour, x0, x1):
        out = []
        for b, near in enumerate(around(v, colour, x0, x1)):
            total = kref[colour, b, 0, x0:x1] * near[0]
            for f in range(1, 6):
                total = total + kref[colour, b, f, x0:x1] * near[f]
            out.append(total)
        return out

    def update(kref, g, v, colour, x0, x1):
        for b, n in enumerate(weigh(kref, v, colour, x0, x1)):
            v[colour, b, x0:x1] = (g[colour, b, x0:x1] + n) * kref[colour, b, 7, x0:x1]

    def first(kref, g, v, x0, x1):
        for b in range(v.shape[1]):
            v[0, b, x0:x1] = g[0, b, x0:x1] * kref[0, b, 7, x0:x1]

    def residual(level, kref, g, v):
        h = ring[level]
        x0, x1 = h, h + own_x[level]
        out = []
        for c in range(2):
            n = weigh(kref, v, c, x0, x1)
            out.append([
                (g[c, b, x0:x1] - (kref[c, b, 6, x0:x1] * v[c, b, x0:x1] - n[b]))[:, h : h + own_y[level]]
                for b in range(len(n))])
        return out

    red_source = [g0.at[0, b] for b in range(2)]
    loads[0].wait()
    dens = unpack(held.at[0])
    place(0, d0, dens)
    dens_one = coarsen(*dens)
    place(1, d1, dens_one)
    loads[1].wait()
    place(0, g0, unpack(held.at[1]))

    beside_x = (gx > 0).astype(jnp.int32) + (gx < nx - 1).astype(jnp.int32)
    beside_y = (gy > 0).astype(jnp.int32) + (gy < ny - 1).astype(jnp.int32)
    pl.semaphore_wait(barrier, nx + ny - 2 + beside_x * beside_y)

    start(1, 0, both(d1))
    start(0, 0, both(d0))
    start(0, 1, red_source)
    dens_two = coarsen(*dens_one)
    inverse = [k1.at[c, 0, 7] for c in range(2)]
    finish(1, 0, both(d1))
    for c in range(2):
        setup(k1, d1, c, 0.25)
    start(1, 1, inverse)
    finish(0, 0, both(d0))
    for c in range(2):
        setup(k0, d0, c, 1.0)
    finish(0, 1, red_source)

    high = 2 + size_x
    first(k0, g0, v0, 1, high + 1)
    update(k0, g0, v0, 1, 2, high)
    for s in range(1, SWEEPS):
        swap(0, 1 + s, black(v0))
        update(k0, g0, v0, 0, 1, high + 1)
        update(k0, g0, v0, 1, 2, high)
    swap(0, 1 + SWEEPS, black(v0), 4)
    place(1, g1, coarsen(*residual(0, k0, g0, v0)))

    start(1, 2, both(g1))
    finish(1, 1, inverse)
    finish(1, 2, both(g1))
    wide = v1.shape[2]
    first(k1, g1, v1, 0, wide)
    for s in range(1, 2 * SWEEPS):
        update(k1, g1, v1, s % 2, s, wide - s)
    start(1, 3, both(v1))
    source_two = coarsen(*residual(1, k1, g1, v1))

    gather(dens_two, source_two)
    for j in range(ny):
        cw[0, :, 2 * j : 2 * j + 2] = gb[j, 0]
        cw[1, :, 2 * j : 2 * j + 2] = gb[j, 1]

    def sides(a):
        plane = jnp.zeros_like(a[:1])
        line = jnp.zeros_like(a[:, :1])
        return (
            jnp.concatenate([plane, a[:-1]], axis=0), jnp.concatenate([a[1:], plane], axis=0),
            row_prev(a, line), row_next(a, line), lane_prev(a), lane_next(a))

    centre = cw[0]
    total = None
    for f, near in enumerate(sides(centre)):
        face = 0.03125 * (centre + near)
        k2[f] = face
        total = face if total is None else total + face
    k2[6] = 1.0 / total
    shape = centre.shape
    red_two = (iota(shape, 0) + iota(shape, 1) + iota(shape, 2)) % 2 == 0
    cw[0] = jnp.zeros(shape, F32)

    def half(red):
        field = cw[0]
        total = cw[1]
        for f, near in enumerate(sides(field)):
            total = total + k2[f] * near
        total = total * k2[6]
        cw[0] = jnp.where(red_two, total, field) if red else jnp.where(red_two, field, total)

    def sweep(i, carry):
        half(True)
        half(False)
        return carry

    lax.fori_loop(0, COARSE_SWEEPS, sweep, 0)
    field = cw[0]
    vc[...] = jnp.zeros(vc.shape, F32)
    for j in range(ny):
        vc[1 + j, 2 : 2 + 2 * nx] = field[:, 2 * j : 2 * j + 2]
    finish(1, 3, both(v1))
    for dy in range(3):
        add = double_rows(vc[gy + dy, pl.ds(2 * gx, 6)])
        for c in range(2):
            v1[c, 0, :, 4 * dy : 4 * dy + 4] = v1[c, 0, :, 4 * dy : 4 * dy + 4] + add
    for s in range(2 * SWEEPS):
        update(k1, g1, v1, s % 2, s + 1, wide - s - 1)

    adds = [double_rows(a) for a in split_even(own(1, v1[0, 0]), own(1, v1[1, 0]))]
    place(0, v0, [adds, adds], add=True)
    for s in range(SWEEPS):
        swap(0, 2 + SWEEPS + s, black(v0))
        update(k0, g0, v0, 0, 1, high + 1)
        update(k0, g0, v0, 1, 2, high)
    start(0, 2 + 2 * SWEEPS, black(v0), 4)
    pack(v_out, *[[own(0, v0[c, b]) for b in range(2)] for c in range(2)])
    finish(0, 2 + 2 * SWEEPS, black(v0), 4)
    pack(r_out, *residual(0, k0, g0, v0))


def solution(mesh):
    nx, ny = mesh.shape["gx"], mesh.shape["gy"]

    def shards(right_side, inverse_density):
        x, y, z = right_side.shape
        p0, p1 = 3 + 2 * SWEEPS, 4

        def halo(phases, fields, own_x, own_y, ring):
            return [
                pltpu.VMEM((phases, 2, fields, ring, own_y, LANES), F32),
                pltpu.VMEM((phases, 2, fields, own_x, ring, LANES), F32),
                pltpu.VMEM((phases, 4, fields, ring, ring, LANES), F32),
            ]

        def level(groups, rows):
            field = pltpu.VMEM((2, groups, rows, REGION_Y, LANES), F32)
            return [pltpu.VMEM((2, groups, 8, rows, REGION_Y, LANES), F32), field, field, field]

        halo0 = halo(p0, 4, x, y, 2)
        halo1 = halo(p1, 2, x // 2, y // 2, 4)
        out = jax.ShapeDtypeStruct(right_side.shape, F32)
        return pl.pallas_call(
            functools.partial(kernel, nx, ny),
            out_shape=(out, out),
            in_specs=[pl.BlockSpec(memory_space=pl.ANY)] * 2,
            out_specs=(pl.BlockSpec(memory_space=pltpu.VMEM),) * 2,
            scratch_shapes=[
                pltpu.VMEM((z, z), jnp.bfloat16),
                *level(2, x + 4),
                *level(1, x // 2 + 8),
                pltpu.VMEM((7, nx * x // 4, ny * y // 4, LANES), F32),
                *halo0, *halo0, *halo1, *halo1,
                pltpu.VMEM((nx, 2, x // 4, y // 4, LANES), F32),
                pltpu.VMEM((ny, 2, nx * x // 4, y // 4, LANES), F32),
                pltpu.VMEM((ny + 2, nx * x // 4 + 4, y // 4, LANES), F32),
                pltpu.VMEM((2, nx * x // 4, ny * y // 4, LANES), F32),
                pltpu.VMEM((2, x, y, z), F32),
                pltpu.SemaphoreType.DMA((2, p0, 8)),
                pltpu.SemaphoreType.DMA((2, p1, 8)),
                pltpu.SemaphoreType.DMA((2, nx)),
                pltpu.SemaphoreType.DMA((2, ny)),
                pltpu.SemaphoreType.DMA((2,)),
            ],
            compiler_params=pltpu.CompilerParams(
                collective_id=0, has_side_effects=True, vmem_limit_bytes=60 * 1024 * 1024
            ),
        )(right_side, inverse_density)

    spec = P("gx", "gy", None)
    return jax.shard_map(shards, mesh=mesh, in_specs=(spec, spec), out_specs=(spec, spec), check_vma=False)
```

```python
import functools

import jax
import jax.numpy as jnp
from jax import lax
from jax.experimental import pallas as pl
from jax.experimental.pallas import tpu as pltpu
from jax.sharding import PartitionSpec as P

SWEEPS = 2
COARSE_SWEEPS = 8
MESH = pl.DeviceIdType.MESH
LANES = 128
F32 = jnp.float32


def iota(shape, dim):
    return lax.broadcasted_iota(jnp.int32, shape, dim)


def lane_prev(a):
    return jnp.where(iota(a.shape, 2) == 0, 0.0, pltpu.roll(a, 1, 2))


def lane_next(a):
    return jnp.where(iota(a.shape, 2) == LANES - 1, 0.0, pltpu.roll(a, LANES - 1, 2))


def row_prev(a, halo):
    return jnp.where(iota(a.shape, 1) == 0, halo, pltpu.roll(a, 1, 1)) if a.shape[1] % 8 == 0 else jnp.concatenate(
        [halo, a[:, :-1]], axis=1
    )


def row_next(a, halo):
    rows = a.shape[1]
    return jnp.where(iota(a.shape, 1) == rows - 1, halo, pltpu.roll(a, rows - 1, 1)) if rows % 8 == 0 else jnp.concatenate(
        [a[:, 1:], halo], axis=1
    )


def even_cells(shape):
    return (iota(shape, 0) + iota(shape, 1)) % 2 == 0


REGION_Y = 16


def z_other(o, colour, first):
    shape = o[0].shape
    even = (iota(shape, 0) + iota(shape, 1)) % 2 == first % 2
    low = even if colour == 0 else jnp.logical_not(even)
    last = len(o) - 1
    out = []
    for b in range(last + 1):
        before = o[b - 1] if b > 0 else lane_prev(o[last])
        after = o[b + 1] if b < last else lane_next(o[0])
        out.append(jnp.where(low, before, after))
    return out


def around(ref, colour, x0, x1):
    other = 1 - colour
    groups = range(ref.shape[1])
    mid = [ref[other, b, x0:x1] for b in groups]
    zo = z_other(mid, colour, x0)
    return [
        (
            ref[other, b, x0 - 1 : x1 - 1],
            ref[other, b, x0 + 1 : x1 + 1],
            pltpu.roll(mid[b], 1, 1),
            pltpu.roll(mid[b], REGION_Y - 1, 1),
            mid[b],
            zo[b],
        )
        for b in groups
    ]


def split_even(zero, one):
    even = even_cells(zero.shape)
    return jnp.where(even, zero, one), jnp.where(even, one, zero)


def pair_rows(a):
    rows = a.shape[1] // 2
    a = a.reshape(a.shape[0] // 2, 2, a.shape[1], LANES)
    a = a[:, 0] + a[:, 1]
    pick = iota((a.shape[0], rows, LANES), 1)
    out = a[:, 0:1] + a[:, 1:2]
    out = jnp.broadcast_to(out, pick.shape)
    for j in range(1, rows):
        out = jnp.where(pick == j, a[:, 2 * j : 2 * j + 1] + a[:, 2 * j + 1 : 2 * j + 2], out)
    return out * 0.125


def double_rows(a):
    x, rows, _ = a.shape
    pick = iota((x, 2 * rows, LANES), 1) // 2
    out = jnp.broadcast_to(a[:, 0:1], pick.shape)
    for j in range(1, rows):
        out = jnp.where(pick == j, a[:, j : j + 1], out)
    return jnp.concatenate([out[i // 2 : i // 2 + 1] for i in range(2 * x)], axis=0)


def three(x):
    high = x.astype(jnp.bfloat16)
    rest = x - high.astype(F32)
    middle = rest.astype(jnp.bfloat16)
    low = (rest - middle.astype(F32)).astype(jnp.bfloat16)
    return high, middle, low


def permute(x, matrix, side):
    parts = [
        lax.dot_general(part, matrix, (((1,), (side,)), ((), ())), preferred_element_type=F32)
        for part in three(x)
    ]
    return (parts[0] + parts[1]) + parts[2]


def kernel(nx, ny, g_ref, c_ref, v_out, r_out, perm, k0, d0, v0, g0, k1, d1, v1, g1, k2,
           sx0, sy0, sc0, rx0, ry0, rc0, sx1, sy1, sc1, rx1, ry1, rc1, ga, gb, vc, cw, held, sem0, sem1, semx, semy, held_sem):
    gx, gy = lax.axis_index("gx"), lax.axis_index("gy")
    send = ((sx0, sy0, sc0), (sx1, sy1, sc1))
    recv = ((rx0, ry0, rc0), (rx1, ry1, rc1))
    sems = (sem0, sem1)
    size_x, size_y = g_ref.shape[:2]
    own_x, own_y, ring = (size_x, size_x // 2), (size_y, size_y // 2), (3, 4)
    near_x = {-1: gx > 0, 0: None, 1: gx < nx - 1}
    near_y = {-1: gy > 0, 0: None, 1: gy < ny - 1}

    ways = []
    for dx, dy in ((-1, 0), (1, 0), (0, -1), (0, 1), (-1, -1), (-1, 1), (1, -1), (1, 1)):
        kind = 2 if dx and dy else (0 if dx else 1)
        side = {0: (dx + 1) // 2, 1: (dy + 1) // 2, 2: (dx + 1) + (dy + 1) // 2}[kind]
        if dx and dy:
            has = jnp.logical_and(near_x[dx], near_y[dy])
        else:
            has = near_x[dx] if dx else near_y[dy]
        target = {}
        if dx:
            target["gx"] = gx + dx
        if dy:
            target["gy"] = gy + dy
        ways.append((dx, dy, kind, side, has, target))
    back = (1, 0, 3, 2, 7, 6, 5, 4)

    loads = [
        pltpu.make_async_copy(ref, held.at[n], held_sem.at[n]) for n, ref in enumerate((c_ref, g_ref))
    ]
    for load in loads:
        load.start()

    barrier = pltpu.get_barrier_semaphore()
    for s in range(1, nx):
        pl.semaphore_signal(barrier, inc=1, device_id={"gx": lax.rem(gx + s, nx)}, device_id_type=MESH)
    for s in range(1, ny):
        pl.semaphore_signal(barrier, inc=1, device_id={"gy": lax.rem(gy + s, ny)}, device_id_type=MESH)
    for dx, dy, kind, side, has, target in ways[4:]:
        @pl.when(has)
        def _():
            pl.semaphore_signal(barrier, inc=1, device_id=target, device_id_type=MESH)

    for level in range(2):
        for dx, dy, kind, side, has, target in ways:
            @pl.when(jnp.logical_not(has))
            def _():
                ref = recv[level][kind]
                ref[:, side] = jnp.zeros((ref.shape[0],) + ref.shape[2:], F32)

    for ref in (d0, v0, g0, d1, v1, g1):
        ref[...] = jnp.zeros(ref.shape, F32)
    for c in range(2):
        k1[c, 0, 7] = jnp.zeros(k1.shape[3:], F32)

    size_z = 4 * LANES
    row, col = iota((size_z, size_z), 0), iota((size_z, size_z), 1)
    perm[...] = (row == 4 * (col % LANES) + col // LANES).astype(F32).astype(jnp.bfloat16)

    def unpack(ref):
        flat = permute(ref[...].reshape(-1, size_z), perm[...], 0)
        quarters = [flat[:, q * LANES : (q + 1) * LANES].reshape(ref.shape[0], ref.shape[1], LANES) for q in range(4)]
        pairs = [split_even(quarters[2 * b], quarters[2 * b + 1]) for b in range(2)]
        return [pairs[b][0] for b in range(2)], [pairs[b][1] for b in range(2)]

    def pack(ref, red, black):
        quarters = []
        for b in range(2):
            quarters.extend(split_even(red[b], black[b]))
        flat = jnp.concatenate([q.reshape(-1, LANES) for q in quarters], axis=1)
        ref[...] = permute(flat, perm[...], 1).reshape(ref.shape)

    def coarsen(red, black):
        pair = [pair_rows(red[b] + black[b]) for b in range(len(red))]
        if len(pair) == 1:
            return pair[0]
        first, second = split_even(pair[0], pair[1])
        return [first], [second]

    def copy(level, ph, d, count, into=False):
        dx, dy, kind, side, has, target = ways[d]
        lands = d if into else back[d]
        sem = sems[level]
        return pltpu.make_async_remote_copy(
            src_ref=send[level][kind].at[ph, side, pl.ds(0, count)],
            dst_ref=recv[level][kind].at[ph, ways[lands][3], pl.ds(0, count)],
            send_sem=sem.at[0, ph, d], recv_sem=sem.at[1, ph, lands], device_id=target, device_id_type=MESH)

    def span(step, own, width, edge):
        if step == 0:
            return slice(width, width + own)
        if edge == "send":
            return slice(width, 2 * width) if step < 0 else slice(own, own + width)
        return slice(0, width) if step < 0 else slice(width + own, 2 * width + own)

    def start(level, ph, fields, count=8):
        x, y, h = own_x[level], own_y[level], ring[level]
        for dx, dy, kind, side, has, target in ways[:count]:
            for f, ref in enumerate(fields):
                send[level][kind][ph, side, f] = ref[span(dx, x, h, "send"), span(dy, y, h, "send"), :]
        for d, way in enumerate(ways[:count]):
            @pl.when(way[4])
            def _():
                copy(level, ph, d, len(fields)).start()

    def finish(level, ph, fields, count=8):
        x, y, h = own_x[level], own_y[level], ring[level]
        for d, way in enumerate(ways[:count]):
            @pl.when(way[4])
            def _():
                copy(level, ph, d, len(fields), into=True).wait_recv()
                copy(level, ph, d, len(fields)).wait_send()
        for dx, dy, kind, side, has, target in ways[:count]:
            for f, ref in enumerate(fields):
                ref[span(dx, x, h, ""), span(dy, y, h, ""), :] = recv[level][kind][ph, side, f]

    def swap(level, ph, fields, count=8):
        start(level, ph, fields, count)
        finish(level, ph, fields, count)

    def both(ref):
        return [ref.at[c, b] for c in range(2) for b in range(ref.shape[1])]

    def black(ref):
        return [ref.at[1, b] for b in range(ref.shape[1])]

    def own(level, a):
        x, y, h = own_x[level], own_y[level], ring[level]
        return a[h : h + x, h : h + y]

    def place(level, ref, fields, add=False):
        x, y, h = own_x[level], own_y[level], ring[level]
        for c in range(2):
            for b, a in enumerate(fields[c]):
                if add:
                    a = a + ref[c, b, h : h + x, h : h + y]
                ref[c, b, h : h + x, h : h + y] = a

    def gather_copy(stage, s):
        if stage == 0:
            return pltpu.make_async_remote_copy(
                src_ref=ga.at[gx], dst_ref=ga.at[gx], send_sem=semx.at[0, s], recv_sem=semx.at[1, s],
                device_id={"gx": lax.rem(gx + s, nx)}, device_id_type=MESH)
        return pltpu.make_async_remote_copy(
            src_ref=gb.at[gy], dst_ref=gb.at[gy], send_sem=semy.at[0, s], recv_sem=semy.at[1, s],
            device_id={"gy": lax.rem(gy + s, ny)}, device_id_type=MESH)

    def gather(dens, source):
        ga[gx, 0] = dens
        ga[gx, 1] = source
        for s in range(1, nx):
            gather_copy(0, s).start()
        for s in range(1, nx):
            src = lax.rem(gx + nx - s, nx)
            pltpu.make_async_remote_copy(
                src_ref=ga.at[src], dst_ref=ga.at[src], send_sem=semx.at[0, s], recv_sem=semx.at[1, s],
                device_id={"gx": src}, device_id_type=MESH).wait_recv()
            gather_copy(0, s).wait_send()
        for i in range(nx):
            gb[gy, 0, 2 * i : 2 * i + 2] = ga[i, 0]
            gb[gy, 1, 2 * i : 2 * i + 2] = ga[i, 1]
        for s in range(1, ny):
            gather_copy(1, s).start()
        for s in range(1, ny):
            src = lax.rem(gy + ny - s, ny)
            pltpu.make_async_remote_copy(
                src_ref=gb.at[src], dst_ref=gb.at[src], send_sem=semy.at[0, s], recv_sem=semy.at[1, s],
                device_id={"gy": src}, device_id_type=MESH).wait_recv()
            gather_copy(1, s).wait_send()

    def setup(kref, dens, colour, scale):
        x0, x1 = 1, dens.shape[2] - 1
        for b, near in enumerate(around(dens, colour, x0, x1)):
            here = dens[colour, b, x0:x1]
            total = None
            for f in range(6):
                face = (scale * 0.5) * (here + near[f])
                kref[colour, b, f, x0:x1] = face
                total = face if total is None else total + face
            kref[colour, b, 6, x0:x1] = total
            kref[colour, b, 7, x0:x1] = jnp.where(here > 0.0, 1.0 / total, 0.0)

    def weigh(kref, v, colour, x0, x1):
        out = []
        for b, near in enumerate(around(v, colour, x0, x1)):
            total = kref[colour, b, 0, x0:x1] * near[0]
            for f in range(1, 6):
                total = total + kref[colour, b, f, x0:x1] * near[f]
            out.append(total)
        return out

    def update(kref, g, v, colour, x0, x1):
        for b, n in enumerate(weigh(kref, v, colour, x0, x1)):
            v[colour, b, x0:x1] = (g[colour, b, x0:x1] + n) * kref[colour, b, 7, x0:x1]

    def first(kref, g, v, x0, x1):
        for b in range(v.shape[1]):
            v[0, b, x0:x1] = g[0, b, x0:x1] * kref[0, b, 7, x0:x1]

    def residual(level, kref, g, v):
        h = ring[level]
        x0, x1 = h, h + own_x[level]
        out = []
        for c in range(2):
            n = weigh(kref, v, c, x0, x1)
            out.append([
                (g[c, b, x0:x1] - (kref[c, b, 6, x0:x1] * v[c, b, x0:x1] - n[b]))[:, h : h + own_y[level]]
                for b in range(len(n))])
        return out

    loads[0].wait()
    dens = unpack(held.at[0])
    place(0, d0, dens)
    dens_one = coarsen(*dens)
    place(1, d1, dens_one)
    loads[1].wait()
    place(0, g0, unpack(held.at[1]))

    beside_x = (gx > 0).astype(jnp.int32) + (gx < nx - 1).astype(jnp.int32)
    beside_y = (gy > 0).astype(jnp.int32) + (gy < ny - 1).astype(jnp.int32)
    pl.semaphore_wait(barrier, nx + ny - 2 + beside_x * beside_y)

    start(1, 0, both(d1))
    start(0, 0, both(d0))
    start(0, 1, both(g0))
    dens_two = coarsen(*dens_one)
    inverse = [k1.at[c, 0, 7] for c in range(2)]
    finish(1, 0, both(d1))
    for c in range(2):
        setup(k1, d1, c, 0.25)
    start(1, 1, inverse)
    finish(0, 0, both(d0))
    for c in range(2):
        setup(k0, d0, c, 1.0)
    finish(0, 1, both(g0))

    low, high = ring[0], ring[0] + size_x

    def fine_sweep(ph, last):
        more = 1 if last else 0
        swap(0, ph, black(v0))
        update(k0, g0, v0, 0, low - 1 - more, high + 1 + more)
        update(k0, g0, v0, 1, low - more, high + more)

    first(k0, g0, v0, low - 1, high + 1)
    update(k0, g0, v0, 1, low, high)
    for s in range(1, SWEEPS):
        fine_sweep(1 + s, s == SWEEPS - 1)
    place(1, g1, coarsen(*residual(0, k0, g0, v0)))

    start(1, 2, both(g1))
    finish(1, 1, inverse)
    finish(1, 2, both(g1))
    wide = v1.shape[2]
    first(k1, g1, v1, 0, wide)
    for s in range(1, 2 * SWEEPS):
        update(k1, g1, v1, s % 2, s, wide - s)
    start(1, 3, both(v1))
    source_two = coarsen(*residual(1, k1, g1, v1))

    gather(dens_two, source_two)
    for j in range(ny):
        cw[0, :, 2 * j : 2 * j + 2] = gb[j, 0]
        cw[1, :, 2 * j : 2 * j + 2] = gb[j, 1]

    def sides(a):
        plane = jnp.zeros_like(a[:1])
        line = jnp.zeros_like(a[:, :1])
        return (
            jnp.concatenate([plane, a[:-1]], axis=0), jnp.concatenate([a[1:], plane], axis=0),
            row_prev(a, line), row_next(a, line), lane_prev(a), lane_next(a))

    centre = cw[0]
    total = None
    for f, near in enumerate(sides(centre)):
        face = 0.03125 * (centre + near)
        k2[f] = face
        total = face if total is None else total + face
    k2[6] = 1.0 / total
    shape = centre.shape
    red_two = (iota(shape, 0) + iota(shape, 1) + iota(shape, 2)) % 2 == 0
    cw[0] = jnp.zeros(shape, F32)

    def half(red):
        field = cw[0]
        total = cw[1]
        for f, near in enumerate(sides(field)):
            total = total + k2[f] * near
        total = total * k2[6]
        cw[0] = jnp.where(red_two, total, field) if red else jnp.where(red_two, field, total)

    def sweep(i, carry):
        half(True)
        half(False)
        return carry

    lax.fori_loop(0, COARSE_SWEEPS, sweep, 0)
    field = cw[0]
    vc[...] = jnp.zeros(vc.shape, F32)
    for j in range(ny):
        vc[1 + j, 2 : 2 + 2 * nx] = field[:, 2 * j : 2 * j + 2]
    finish(1, 3, both(v1))
    for dy in range(3):
        add = double_rows(vc[gy + dy, pl.ds(2 * gx, 6)])
        for c in range(2):
            v1[c, 0, :, 4 * dy : 4 * dy + 4] = v1[c, 0, :, 4 * dy : 4 * dy + 4] + add
    for s in range(2 * SWEEPS):
        update(k1, g1, v1, s % 2, s + 1, wide - s - 1)

    adds = [double_rows(a) for a in split_even(own(1, v1[0, 0]), own(1, v1[1, 0]))]
    place(0, v0, [adds, adds], add=True)
    for s in range(SWEEPS):
        fine_sweep(2 + SWEEPS + s, s == SWEEPS - 1)
    pack(v_out, *[[own(0, v0[c, b]) for b in range(2)] for c in range(2)])
    pack(r_out, *residual(0, k0, g0, v0))


def solution(mesh):
    nx, ny = mesh.shape["gx"], mesh.shape["gy"]

    def shards(right_side, inverse_density):
        x, y, z = right_side.shape
        p0, p1 = 3 + 2 * SWEEPS, 4

        def halo(phases, fields, own_x, own_y, ring):
            return [
                pltpu.VMEM((phases, 2, fields, ring, own_y, LANES), F32),
                pltpu.VMEM((phases, 2, fields, own_x, ring, LANES), F32),
                pltpu.VMEM((phases, 4, fields, ring, ring, LANES), F32),
            ]

        def level(groups, rows):
            field = pltpu.VMEM((2, groups, rows, REGION_Y, LANES), F32)
            return [pltpu.VMEM((2, groups, 8, rows, REGION_Y, LANES), F32), field, field, field]

        halo0 = halo(p0, 4, x, y, 3)
        halo1 = halo(p1, 2, x // 2, y // 2, 4)
        out = jax.ShapeDtypeStruct(right_side.shape, F32)
        return pl.pallas_call(
            functools.partial(kernel, nx, ny),
            out_shape=(out, out),
            in_specs=[pl.BlockSpec(memory_space=pl.ANY)] * 2,
            out_specs=(pl.BlockSpec(memory_space=pltpu.VMEM),) * 2,
            scratch_shapes=[
                pltpu.VMEM((z, z), jnp.bfloat16),
                *level(2, x + 6),
                *level(1, x // 2 + 8),
                pltpu.VMEM((7, nx * x // 4, ny * y // 4, LANES), F32),
                *halo0, *halo0, *halo1, *halo1,
                pltpu.VMEM((nx, 2, x // 4, y // 4, LANES), F32),
                pltpu.VMEM((ny, 2, nx * x // 4, y // 4, LANES), F32),
                pltpu.VMEM((ny + 2, nx * x // 4 + 4, y // 4, LANES), F32),
                pltpu.VMEM((2, nx * x // 4, ny * y // 4, LANES), F32),
                pltpu.VMEM((2, x, y, z), F32),
                pltpu.SemaphoreType.DMA((2, p0, 8)),
                pltpu.SemaphoreType.DMA((2, p1, 8)),
                pltpu.SemaphoreType.DMA((2, nx)),
                pltpu.SemaphoreType.DMA((2, ny)),
                pltpu.SemaphoreType.DMA((2,)),
            ],
            compiler_params=pltpu.CompilerParams(
                collective_id=0, has_side_effects=True, vmem_limit_bytes=60 * 1024 * 1024
            ),
        )(right_side, inverse_density)

    spec = P("gx", "gy", None)
    return jax.shard_map(shards, mesh=mesh, in_specs=(spec, spec), out_specs=(spec, spec), check_vma=False)
```

```python
import functools

import jax
import jax.numpy as jnp
from jax import lax
from jax.experimental import pallas as pl
from jax.experimental.pallas import tpu as pltpu
from jax.sharding import PartitionSpec as P

SWEEPS = 2
COARSE_SWEEPS = 8
MESH = pl.DeviceIdType.MESH
LANES = 128
F32 = jnp.float32


def iota(shape, dim):
    return lax.broadcasted_iota(jnp.int32, shape, dim)


def lane_prev(a):
    return jnp.where(iota(a.shape, 2) == 0, 0.0, pltpu.roll(a, 1, 2))


def lane_next(a):
    return jnp.where(iota(a.shape, 2) == LANES - 1, 0.0, pltpu.roll(a, LANES - 1, 2))


def row_prev(a, halo):
    return jnp.where(iota(a.shape, 1) == 0, halo, pltpu.roll(a, 1, 1)) if a.shape[1] % 8 == 0 else jnp.concatenate(
        [halo, a[:, :-1]], axis=1
    )


def row_next(a, halo):
    rows = a.shape[1]
    return jnp.where(iota(a.shape, 1) == rows - 1, halo, pltpu.roll(a, rows - 1, 1)) if rows % 8 == 0 else jnp.concatenate(
        [a[:, 1:], halo], axis=1
    )


def even_cells(shape):
    return (iota(shape, 0) + iota(shape, 1)) % 2 == 0


REGION_Y = 16


def z_other(o, colour, first):
    shape = o[0].shape
    even = (iota(shape, 0) + iota(shape, 1)) % 2 == first % 2
    low = even if colour == 0 else jnp.logical_not(even)
    last = len(o) - 1
    out = []
    for b in range(last + 1):
        before = o[b - 1] if b > 0 else lane_prev(o[last])
        after = o[b + 1] if b < last else lane_next(o[0])
        out.append(jnp.where(low, before, after))
    return out


def around(ref, colour, x0, x1):
    other = 1 - colour
    groups = range(ref.shape[1])
    mid = [ref[other, b, x0:x1] for b in groups]
    zo = z_other(mid, colour, x0)
    return [
        (
            ref[other, b, x0 - 1 : x1 - 1],
            ref[other, b, x0 + 1 : x1 + 1],
            pltpu.roll(mid[b], 1, 1),
            pltpu.roll(mid[b], REGION_Y - 1, 1),
            mid[b],
            zo[b],
        )
        for b in groups
    ]


def split_even(zero, one):
    even = even_cells(zero.shape)
    return jnp.where(even, zero, one), jnp.where(even, one, zero)


def pair_rows(a):
    rows = a.shape[1] // 2
    a = a.reshape(a.shape[0] // 2, 2, a.shape[1], LANES)
    a = a[:, 0] + a[:, 1]
    pick = iota((a.shape[0], rows, LANES), 1)
    out = a[:, 0:1] + a[:, 1:2]
    out = jnp.broadcast_to(out, pick.shape)
    for j in range(1, rows):
        out = jnp.where(pick == j, a[:, 2 * j : 2 * j + 1] + a[:, 2 * j + 1 : 2 * j + 2], out)
    return out * 0.125


def double_rows(a):
    x, rows, _ = a.shape
    pick = iota((x, 2 * rows, LANES), 1) // 2
    out = jnp.broadcast_to(a[:, 0:1], pick.shape)
    for j in range(1, rows):
        out = jnp.where(pick == j, a[:, j : j + 1], out)
    return jnp.concatenate([out[i // 2 : i // 2 + 1] for i in range(2 * x)], axis=0)


def three(x):
    high = x.astype(jnp.bfloat16)
    rest = x - high.astype(F32)
    middle = rest.astype(jnp.bfloat16)
    low = (rest - middle.astype(F32)).astype(jnp.bfloat16)
    return high, middle, low


def permute(x, matrix, side):
    parts = [
        lax.dot_general(part, matrix, (((1,), (side,)), ((), ())), preferred_element_type=F32)
        for part in three(x)
    ]
    return (parts[0] + parts[1]) + parts[2]


def kernel(nx, ny, g_ref, c_ref, v_out, r_out, perm, k0, d0, v0, g0, k1, d1, v1, g1, k2,
           sx0, sy0, sc0, rx0, ry0, rc0, sx1, sy1, sc1, rx1, ry1, rc1, ga, vc, cw, held, sem0, sem1, sem_all, held_sem):
    gx, gy = lax.axis_index("gx"), lax.axis_index("gy")
    send = ((sx0, sy0, sc0), (sx1, sy1, sc1))
    recv = ((rx0, ry0, rc0), (rx1, ry1, rc1))
    sems = (sem0, sem1)
    size_x, size_y = g_ref.shape[:2]
    own_x, own_y, ring = (size_x, size_x // 2), (size_y, size_y // 2), (3, 4)
    near_x = {-1: gx > 0, 0: None, 1: gx < nx - 1}
    near_y = {-1: gy > 0, 0: None, 1: gy < ny - 1}

    ways = []
    for dx, dy in ((-1, 0), (1, 0), (0, -1), (0, 1), (-1, -1), (-1, 1), (1, -1), (1, 1)):
        kind = 2 if dx and dy else (0 if dx else 1)
        side = {0: (dx + 1) // 2, 1: (dy + 1) // 2, 2: (dx + 1) + (dy + 1) // 2}[kind]
        if dx and dy:
            has = jnp.logical_and(near_x[dx], near_y[dy])
        else:
            has = near_x[dx] if dx else near_y[dy]
        target = {}
        if dx:
            target["gx"] = gx + dx
        if dy:
            target["gy"] = gy + dy
        ways.append((dx, dy, kind, side, has, target))
    back = (1, 0, 3, 2, 7, 6, 5, 4)

    loads = [
        pltpu.make_async_copy(ref, held.at[n], held_sem.at[n]) for n, ref in enumerate((c_ref, g_ref))
    ]
    for load in loads:
        load.start()

    barrier = pltpu.get_barrier_semaphore()
    others = [(a, b) for b in range(ny) for a in range(nx) if a or b]
    for a, b in others:
        target = {"gx": lax.rem(gx + a, nx), "gy": lax.rem(gy + b, ny)}
        pl.semaphore_signal(barrier, inc=1, device_id=target, device_id_type=MESH)

    for level in range(2):
        for dx, dy, kind, side, has, target in ways:
            @pl.when(jnp.logical_not(has))
            def _():
                ref = recv[level][kind]
                ref[:, side] = jnp.zeros((ref.shape[0],) + ref.shape[2:], F32)

    for ref in (d0, v0, g0, d1, v1, g1):
        ref[...] = jnp.zeros(ref.shape, F32)
    for c in range(2):
        k1[c, 0, 7] = jnp.zeros(k1.shape[3:], F32)

    size_z = 4 * LANES
    row, col = iota((size_z, size_z), 0), iota((size_z, size_z), 1)
    perm[...] = (row == 4 * (col % LANES) + col // LANES).astype(F32).astype(jnp.bfloat16)

    def unpack(ref):
        flat = permute(ref[...].reshape(-1, size_z), perm[...], 0)
        quarters = [flat[:, q * LANES : (q + 1) * LANES].reshape(ref.shape[0], ref.shape[1], LANES) for q in range(4)]
        pairs = [split_even(quarters[2 * b], quarters[2 * b + 1]) for b in range(2)]
        return [pairs[b][0] for b in range(2)], [pairs[b][1] for b in range(2)]

    def pack(ref, red, black):
        quarters = []
        for b in range(2):
            quarters.extend(split_even(red[b], black[b]))
        flat = jnp.concatenate([q.reshape(-1, LANES) for q in quarters], axis=1)
        ref[...] = permute(flat, perm[...], 1).reshape(ref.shape)

    def coarsen(red, black):
        pair = [pair_rows(red[b] + black[b]) for b in range(len(red))]
        if len(pair) == 1:
            return pair[0]
        first, second = split_even(pair[0], pair[1])
        return [first], [second]

    def copy(level, ph, d, count, into=False):
        dx, dy, kind, side, has, target = ways[d]
        lands = d if into else back[d]
        sem = sems[level]
        return pltpu.make_async_remote_copy(
            src_ref=send[level][kind].at[ph, side, pl.ds(0, count)],
            dst_ref=recv[level][kind].at[ph, ways[lands][3], pl.ds(0, count)],
            send_sem=sem.at[0, ph, d], recv_sem=sem.at[1, ph, lands], device_id=target, device_id_type=MESH)

    def span(step, own, width, edge):
        if step == 0:
            return slice(width, width + own)
        if edge == "send":
            return slice(width, 2 * width) if step < 0 else slice(own, own + width)
        return slice(0, width) if step < 0 else slice(width + own, 2 * width + own)

    def start(level, ph, fields, count=8):
        x, y, h = own_x[level], own_y[level], ring[level]
        for dx, dy, kind, side, has, target in ways[:count]:
            for f, ref in enumerate(fields):
                send[level][kind][ph, side, f] = ref[span(dx, x, h, "send"), span(dy, y, h, "send"), :]
        for d, way in enumerate(ways[:count]):
            @pl.when(way[4])
            def _():
                copy(level, ph, d, len(fields)).start()

    def finish(level, ph, fields, count=8):
        x, y, h = own_x[level], own_y[level], ring[level]
        for d, way in enumerate(ways[:count]):
            @pl.when(way[4])
            def _():
                copy(level, ph, d, len(fields), into=True).wait_recv()
        sent.append((level, ph, len(fields)))
        for dx, dy, kind, side, has, target in ways[:count]:
            for f, ref in enumerate(fields):
                ref[span(dx, x, h, ""), span(dy, y, h, ""), :] = recv[level][kind][ph, side, f]

    sent = []

    def swap(level, ph, fields, count=8):
        start(level, ph, fields, count)
        finish(level, ph, fields, count)

    def both(ref):
        return [ref.at[c, b] for c in range(2) for b in range(ref.shape[1])]

    def black(ref):
        return [ref.at[1, b] for b in range(ref.shape[1])]

    def own(level, a):
        x, y, h = own_x[level], own_y[level], ring[level]
        return a[h : h + x, h : h + y]

    def place(level, ref, fields, add=False):
        x, y, h = own_x[level], own_y[level], ring[level]
        for c in range(2):
            for b, a in enumerate(fields[c]):
                if add:
                    a = a + ref[c, b, h : h + x, h : h + y]
                ref[c, b, h : h + x, h : h + y] = a

    def gather_copy(a, b, into=False):
        slot = ga.at[lax.rem(gy + ny - b, ny), lax.rem(gx + nx - a, nx)] if into else ga.at[gy, gx]
        return pltpu.make_async_remote_copy(
            src_ref=slot, dst_ref=slot, send_sem=sem_all.at[0, b, a], recv_sem=sem_all.at[1, b, a],
            device_id={"gx": lax.rem(gx + a, nx), "gy": lax.rem(gy + b, ny)}, device_id_type=MESH)

    def gather(dens, source):
        ga[gy, gx, 0] = dens
        ga[gy, gx, 1] = source
        for a, b in reversed(others):
            gather_copy(a, b).start()
        for a, b in reversed(others):
            gather_copy(a, b, into=True).wait_recv()

    def setup(kref, dens, colour, scale):
        x0, x1 = 1, dens.shape[2] - 1
        for b, near in enumerate(around(dens, colour, x0, x1)):
            here = dens[colour, b, x0:x1]
            total = None
            for f in range(6):
                face = (scale * 0.5) * (here + near[f])
                kref[colour, b, f, x0:x1] = face
                total = face if total is None else total + face
            kref[colour, b, 6, x0:x1] = total
            kref[colour, b, 7, x0:x1] = jnp.where(here > 0.0, 1.0 / total, 0.0)

    def weigh(kref, v, colour, x0, x1):
        out = []
        for b, near in enumerate(around(v, colour, x0, x1)):
            total = kref[colour, b, 0, x0:x1] * near[0]
            for f in range(1, 6):
                total = total + kref[colour, b, f, x0:x1] * near[f]
            out.append(total)
        return out

    def update(kref, g, v, colour, x0, x1):
        for b, n in enumerate(weigh(kref, v, colour, x0, x1)):
            v[colour, b, x0:x1] = (g[colour, b, x0:x1] + n) * kref[colour, b, 7, x0:x1]

    def first(kref, g, v, x0, x1):
        for b in range(v.shape[1]):
            v[0, b, x0:x1] = g[0, b, x0:x1] * kref[0, b, 7, x0:x1]

    def residual(level, kref, g, v):
        h = ring[level]
        x0, x1 = h, h + own_x[level]
        out = []
        for c in range(2):
            n = weigh(kref, v, c, x0, x1)
            out.append([
                (g[c, b, x0:x1] - (kref[c, b, 6, x0:x1] * v[c, b, x0:x1] - n[b]))[:, h : h + own_y[level]]
                for b in range(len(n))])
        return out

    loads[0].wait()
    dens = unpack(held.at[0])
    place(0, d0, dens)
    dens_one = coarsen(*dens)
    place(1, d1, dens_one)
    loads[1].wait()
    place(0, g0, unpack(held.at[1]))

    pl.semaphore_wait(barrier, nx * ny - 1)

    start(1, 0, both(d1))
    start(0, 0, both(d0))
    start(0, 1, both(g0))
    dens_two = coarsen(*dens_one)
    inverse = [k1.at[c, 0, 7] for c in range(2)]
    finish(1, 0, both(d1))
    for c in range(2):
        setup(k1, d1, c, 0.25)
    start(1, 1, inverse)
    finish(0, 0, both(d0))
    for c in range(2):
        setup(k0, d0, c, 1.0)
    finish(0, 1, both(g0))

    low, high = ring[0], ring[0] + size_x

    def fine_sweep(ph, last):
        more = 1 if last else 0
        swap(0, ph, black(v0))
        update(k0, g0, v0, 0, low - 1 - more, high + 1 + more)
        update(k0, g0, v0, 1, low - more, high + more)

    first(k0, g0, v0, low - 1, high + 1)
    update(k0, g0, v0, 1, low, high)
    for s in range(1, SWEEPS):
        fine_sweep(1 + s, s == SWEEPS - 1)
    place(1, g1, coarsen(*residual(0, k0, g0, v0)))

    start(1, 2, both(g1))
    finish(1, 1, inverse)
    finish(1, 2, both(g1))
    wide = v1.shape[2]
    first(k1, g1, v1, 0, wide)
    for s in range(1, 2 * SWEEPS):
        update(k1, g1, v1, s % 2, s, wide - s)
    start(1, 3, both(v1))
    source_two = coarsen(*residual(1, k1, g1, v1))

    gather(dens_two, source_two)
    for j in range(ny):
        for i in range(nx):
            for n in range(2):
                cw[n, 2 * i : 2 * i + 2, 2 * j : 2 * j + 2] = ga[j, i, n]

    def sides(a):
        plane = jnp.zeros_like(a[:1])
        line = jnp.zeros_like(a[:, :1])
        return (
            jnp.concatenate([plane, a[:-1]], axis=0), jnp.concatenate([a[1:], plane], axis=0),
            row_prev(a, line), row_next(a, line), lane_prev(a), lane_next(a))

    centre = cw[0]
    total = None
    for f, near in enumerate(sides(centre)):
        face = 0.03125 * (centre + near)
        k2[f] = face
        total = face if total is None else total + face
    k2[6] = 1.0 / total
    shape = centre.shape
    red_two = (iota(shape, 0) + iota(shape, 1) + iota(shape, 2)) % 2 == 0
    cw[0] = jnp.zeros(shape, F32)

    def half(red):
        field = cw[0]
        total = cw[1]
        for f, near in enumerate(sides(field)):
            total = total + k2[f] * near
        total = total * k2[6]
        cw[0] = jnp.where(red_two, total, field) if red else jnp.where(red_two, field, total)

    def sweep(i, carry):
        half(True)
        half(False)
        return carry

    lax.fori_loop(0, COARSE_SWEEPS, sweep, 0)
    field = cw[0]
    vc[...] = jnp.zeros(vc.shape, F32)
    for j in range(ny):
        vc[1 + j, 2 : 2 + 2 * nx] = field[:, 2 * j : 2 * j + 2]
    finish(1, 3, both(v1))
    for dy in range(3):
        add = double_rows(vc[gy + dy, pl.ds(2 * gx, 6)])
        for c in range(2):
            v1[c, 0, :, 4 * dy : 4 * dy + 4] = v1[c, 0, :, 4 * dy : 4 * dy + 4] + add
    for s in range(2 * SWEEPS):
        update(k1, g1, v1, s % 2, s + 1, wide - s - 1)

    adds = [double_rows(a) for a in split_even(own(1, v1[0, 0]), own(1, v1[1, 0]))]
    place(0, v0, [adds, adds], add=True)
    for s in range(SWEEPS):
        fine_sweep(2 + SWEEPS + s, s == SWEEPS - 1)
    pack(v_out, *[[own(0, v0[c, b]) for b in range(2)] for c in range(2)])
    pack(r_out, *residual(0, k0, g0, v0))
    for d, way in enumerate(ways):
        @pl.when(way[4])
        def _():
            for level, ph, fields in sent:
                copy(level, ph, d, fields).wait_send()
    for a, b in others:
        gather_copy(a, b).wait_send()


def solution(mesh):
    nx, ny = mesh.shape["gx"], mesh.shape["gy"]

    def shards(right_side, inverse_density):
        x, y, z = right_side.shape
        p0, p1 = 3 + 2 * SWEEPS, 4

        def halo(phases, fields, own_x, own_y, ring):
            return [
                pltpu.VMEM((phases, 2, fields, ring, own_y, LANES), F32),
                pltpu.VMEM((phases, 2, fields, own_x, ring, LANES), F32),
                pltpu.VMEM((phases, 4, fields, ring, ring, LANES), F32),
            ]

        def level(groups, rows):
            field = pltpu.VMEM((2, groups, rows, REGION_Y, LANES), F32)
            return [pltpu.VMEM((2, groups, 8, rows, REGION_Y, LANES), F32), field, field, field]

        halo0 = halo(p0, 4, x, y, 3)
        halo1 = halo(p1, 2, x // 2, y // 2, 4)
        out = jax.ShapeDtypeStruct(right_side.shape, F32)
        return pl.pallas_call(
            functools.partial(kernel, nx, ny),
            out_shape=(out, out),
            in_specs=[pl.BlockSpec(memory_space=pl.ANY)] * 2,
            out_specs=(pl.BlockSpec(memory_space=pltpu.VMEM),) * 2,
            scratch_shapes=[
                pltpu.VMEM((z, z), jnp.bfloat16),
                *level(2, x + 6),
                *level(1, x // 2 + 8),
                pltpu.VMEM((7, nx * x // 4, ny * y // 4, LANES), F32),
                *halo0, *halo0, *halo1, *halo1,
                pltpu.VMEM((ny, nx, 2, x // 4, y // 4, LANES), F32),
                pltpu.VMEM((ny + 2, nx * x // 4 + 4, y // 4, LANES), F32),
                pltpu.VMEM((2, nx * x // 4, ny * y // 4, LANES), F32),
                pltpu.VMEM((2, x, y, z), F32),
                pltpu.SemaphoreType.DMA((2, p0, 8)),
                pltpu.SemaphoreType.DMA((2, p1, 8)),
                pltpu.SemaphoreType.DMA((2, ny, nx)),
                pltpu.SemaphoreType.DMA((2,)),
            ],
            compiler_params=pltpu.CompilerParams(
                collective_id=0, has_side_effects=True, vmem_limit_bytes=60 * 1024 * 1024
            ),
        )(right_side, inverse_density)

    spec = P("gx", "gy", None)
    return jax.shard_map(shards, mesh=mesh, in_specs=(spec, spec), out_specs=(spec, spec), check_vma=False)
```
